512 devices in a mesh: cells: 64 (over z, x_lo, core), nets: 8 (over x_hi, y).
Axes of the slice: x: 4 (x_hi: 2, x_lo: 2; x = x_hi * 2 + x_lo), y: 4, z: 16, core: 2. Of those that a mesh axis runs over, the one named last changes fastest.
Arguments:
- grad_out: bfloat16 [131072, 512], P(('cells', 'nets')), may hold values from -6 to 6
- saved_agg: bfloat16 [131072, 512], P(('cells', 'nets')), may hold values from -0.015625 to 0.015625
- theta: bfloat16 [512, 512], replicated, may hold values from -0.25 to 0.25
- tile_values: bfloat16 [64, 8, 16, 128, 128], P('cells', 'nets'), may hold values from -0.5 to 0.5
- tile_coords: int32 [64, 8, 16, 2], P('cells', 'nets'), may hold values from 0 to 15, as said below
- block_tile_count: int32 [64, 8], P('cells', 'nets'), may hold values from 4 to 16, as said below
- cell_degree: int32 [131072], P('cells'), may hold values from 1 to 8
- net_pin_count: int32 [8192], P('nets'), may hold values from 12 to 39
Outputs:
- grad_cells: bfloat16 [131072, 512], P(('cells', 'nets'))
- layer_weight_gradient: bfloat16 [512, 512], replicated
The draws below stay inside these ranges and needn't reach their ends.
Inputs may be any that keep to these rules, and one draw needn't show every extreme that they name: `tile_coords`: within each block the 16 slots name distinct tiles: column 0 a cell tile below 16, column 1 a net tile below 8. Slots at and beyond the block's count carry no weight. `block_tile_count`: live slots of each block are its first ones; some block of every draw has all 16 live.
All inputs are finite; a program needn't handle non-finite values.
Results may differ from the reference program's by a relative error of at most 0.015.
Values may be sent and summed in bfloat16 or wider, within the bound.
No kernel may reach another device: no remote copies, remote signals or barrier semaphores. Data moves between devices by JAX's collectives and lax.ppermute only.
A program may use at most 64 MiB of HBM per device.

```python
import jax
import jax.numpy as jnp
from jax import lax

D = 512
TILE = 128
CBLK = 2048
NBLK = 1024
TILES_DEV = 16
NC = 131072
NE = 8192
N_CELLS = 64
N_NETS = 8


def draw_tile_coords(key, part):
    net_tiles = NBLK // TILE
    slot_total = CBLK // TILE * net_tiles
    block_keys = jax.random.split(key, N_CELLS * N_NETS)
    chosen = jax.vmap(lambda block_key: jax.random.permutation(block_key, slot_total)[:TILES_DEV])(block_keys)
    chosen = chosen.astype(jnp.int32).reshape(N_CELLS, N_NETS, TILES_DEV)
    return jnp.stack([chosen // net_tiles, chosen % net_tiles], axis=-1).astype(jnp.int32)


def draw_block_tile_count(key, part):
    level = jax.random.randint(key, (N_CELLS * N_NETS,), 1, 5)
    counts = TILES_DEV // level
    chosen_block = jax.random.randint(jax.random.fold_in(key, 7), (), 0, N_CELLS * N_NETS)
    counts = jnp.where(jnp.arange(N_CELLS * N_NETS) == chosen_block, TILES_DEV, counts)
    return counts.reshape(N_CELLS, N_NETS).astype(jnp.int32)


def with_ends(result, rng, smallest, largest):
    shape = result.shape
    place = [jax.random.randint(jax.random.fold_in(rng, axis), (), 0, shape[axis]) for axis in range(len(shape))]
    result = result.at[tuple(place)].set(smallest)
    longest = shape.index(max(shape))
    place[longest] = (place[longest] + 1) % shape[longest]
    return result.at[tuple(place)].set(largest)


def block_scale(rng, dims, cuts, smallest, largest):
    def one(dim, blocks):
        steps = jax.random.uniform(jax.random.fold_in(jax.random.fold_in(rng, 6), dim), (blocks,), jnp.float32, smallest / len(cuts), largest / len(cuts))
        return jnp.repeat(jnp.exp(steps), dims[dim] // blocks).reshape((-1,) + (1,) * (len(dims) - dim - 1))

    loudness = one(*cuts[0])
    for cut in cuts[1:]:
        loudness = loudness * one(*cut)
    return loudness


def bell_draw(stream_key, extent, width, most, shards=(), held_as=jnp.bfloat16):
    drawn = jax.random.normal(stream_key, extent, jnp.float32) * width
    if len(shards) > 0:
        drawn = block_scale(stream_key, extent, shards, -0.22, 0.18) * drawn
    return jnp.clip(drawn, min=-most, max=most).astype(held_as)


def setup_inputs(seed: int = 0) -> dict:
    key_list = jax.random.split(jax.random.key(seed), 9)
    return {
        "grad_out": bell_draw(key_list[0], (NC, D), 1.0, 6.0, ((0, 512),)),
        "saved_agg": bell_draw(key_list[1], (NC, D), NC ** -0.5, 0.015625, ((0, 512),)),
        "theta": bell_draw(key_list[2], (D, D), D ** -0.5, 0.25),
        "tile_values": bell_draw(key_list[3], (N_CELLS, N_NETS, TILES_DEV, TILE, TILE), TILE ** -0.5, 0.5, ((0, 64), (1, 8))),
        "tile_coords": draw_tile_coords(jax.random.fold_in(key_list[8], 71), 0),
        "block_tile_count": draw_block_tile_count(jax.random.fold_in(key_list[8], 71), 0),
        "cell_degree": with_ends(jax.random.randint(key_list[6], (NC,), 1, 9), jax.random.fold_in(key_list[6], 1), 1, 8).astype(jnp.int32),
        "net_pin_count": with_ends(jax.random.randint(key_list[7], (NE,), 12, 40), jax.random.fold_in(key_list[7], 1), 12, 39).astype(jnp.int32),
    }


def dense_block(tile_vals, coords, live_count):
    cell_tiles = CBLK // TILE
    net_tiles = NBLK // TILE
    live_mask = jnp.arange(TILES_DEV, dtype=jnp.int32) < live_count
    row_pick = ((coords[:, 0:1] == jnp.arange(cell_tiles, dtype=jnp.int32)[None, :]) & live_mask[:, None]).astype(jnp.float32)
    col_pick = (coords[:, 1:2] == jnp.arange(net_tiles, dtype=jnp.int32)[None, :]).astype(jnp.float32)
    dense = jnp.einsum('tr,tc,tmk->rmck', row_pick, col_pick, tile_vals.astype(jnp.float32))
    return dense.reshape(CBLK, NBLK).astype(jnp.bfloat16)

def reference(grad_out, saved_agg, theta, tile_values, tile_coords, block_tile_count, cell_degree, net_pin_count):
    grad_z = jnp.dot(grad_out, theta.T, preferred_element_type=jnp.float32)
    cell_root = jnp.sqrt(cell_degree.astype(jnp.float32))[:, None]
    scaled = (grad_z / cell_root).astype(jnp.bfloat16).reshape(N_CELLS, CBLK, D)

    def net_step(running, inputs):
        block_entries_list, block_coords, block_counts, block_rows = inputs

        def one_block(tile_vals, coords, live_count):
            return jnp.dot(dense_block(tile_vals, coords, live_count).T, block_rows, preferred_element_type=jnp.float32)
        return (running + jax.vmap(one_block)(block_entries_list, block_coords, block_counts), None)
    net_sum, _ = lax.scan(net_step, jnp.zeros((N_NETS, NBLK, D), jnp.float32), (tile_values, tile_coords, block_tile_count, scaled))
    net_grad = (net_sum / net_pin_count.reshape(N_NETS, NBLK, 1).astype(jnp.float32)).astype(jnp.bfloat16)

    def cell_block(inputs):
        block_entries_list, block_coords, block_counts = inputs

        def one_block(tile_vals, coords, live_count, net_rows):
            return jnp.dot(dense_block(tile_vals, coords, live_count), net_rows, preferred_element_type=jnp.float32).astype(jnp.bfloat16)
        partials = jax.vmap(one_block)(block_entries_list, block_coords, block_counts, net_grad)
        return lax.optimization_barrier(jnp.sum(partials.astype(jnp.float32), axis=0))
    cell_sum = lax.map(cell_block, (tile_values, tile_coords, block_tile_count)).reshape(N_CELLS * CBLK, D)
    grad_cells = (cell_sum / cell_root).astype(jnp.bfloat16)
    layer_weight_gradient = jnp.dot(saved_agg.T, grad_out, preferred_element_type=jnp.float32).astype(jnp.bfloat16)
    return (grad_cells, layer_weight_gradient)
```

```python
import jax
import jax.numpy as jnp
from jax import lax
from jax.experimental import pallas as pl
from jax.experimental.pallas import tpu as pltpu
from jax.sharding import Mesh
from jax.sharding import PartitionSpec as P

SWAP = ((0, 1), (1, 0))
CELLS = ("z", "xl", "core")
NETS = ("xh", "y")


def dense_kernel(coords_ref, count_ref, tiles_ref, out_ref):
    out_ref[...] = jnp.zeros_like(out_ref)
    slots, tile_len, _ = tiles_ref.shape
    for t in range(slots):

        @pl.when(t < count_ref[0])
        def _():
            row = pl.multiple_of(coords_ref[t, 0] * tile_len, tile_len)
            column = pl.multiple_of(coords_ref[t, 1] * tile_len, tile_len)
            out_ref[pl.ds(row, tile_len), pl.ds(column, tile_len)] = tiles_ref[t]


def dense_block(tiles, coords, count, cells, nets):
    return pl.pallas_call(
        dense_kernel,
        out_shape=jax.ShapeDtypeStruct((cells, nets), tiles.dtype),
        in_specs=[
            pl.BlockSpec(memory_space=pltpu.SMEM),
            pl.BlockSpec(memory_space=pltpu.SMEM),
            pl.BlockSpec(memory_space=pltpu.VMEM),
        ],
        out_specs=pl.BlockSpec(memory_space=pltpu.VMEM),
        compiler_params=pltpu.CompilerParams(vmem_limit_bytes=16 << 20),
        cost_estimate=pl.CostEstimate(flops=0, bytes_accessed=10 << 20, transcendentals=0),
        name="dense_block",
    )(coords, count, tiles)


def half(x, which):
    rows = x.shape[0] // 2
    return lax.dynamic_slice_in_dim(x, which * rows, rows)


def fold_pair(x, axis):
    me = lax.axis_index(axis)
    sent = half(x, 1 - me).astype(jnp.bfloat16)
    return half(x, me) + lax.ppermute(sent, axis, SWAP).astype(jnp.float32)


def join_pair(x, axis):
    other = lax.ppermute(x, axis, SWAP)
    first = lax.axis_index(axis) == 0
    return jnp.concatenate([jnp.where(first, x, other), jnp.where(first, other, x)], axis=0)


def spread(x, axes):
    n = lax.axis_size(axes)
    copies = jnp.broadcast_to(x[None], (n,) + x.shape)
    return lax.all_to_all(copies, axes, 0, 0).reshape((n * x.shape[0],) + x.shape[1:])


def fold(x, axes):
    n = lax.axis_size(axes)
    terms = x.astype(jnp.bfloat16).reshape((n, x.shape[0] // n) + x.shape[1:])
    return jnp.sum(lax.all_to_all(terms, axes, 0, 0).astype(jnp.float32), axis=0)


def shards(
    grad_out,
    saved_agg,
    theta,
    tile_values,
    tile_coords,
    block_tile_count,
    cell_degree,
    net_pin_count,
):
    own_rows = grad_out.shape[0]
    block_cells = cell_degree.shape[0]
    block_nets = net_pin_count.shape[0]
    net_position = lax.axis_index(NETS)
    own_degree = lax.dynamic_slice_in_dim(cell_degree, net_position * own_rows, own_rows)
    own_root = jnp.sqrt(own_degree.astype(jnp.float32))[:, None]
    grad_z = lax.dot_general(
        grad_out, theta, (((1,), (1,)), ((), ())), preferred_element_type=jnp.float32
    )
    scaled = (grad_z / own_root).astype(jnp.bfloat16)
    gathered = spread(scaled, NETS)

    block = dense_block(
        tile_values[0, 0], tile_coords[0, 0], block_tile_count[0], block_cells, block_nets
    )

    weight_term = lax.dot_general(
        saved_agg, grad_out, (((0,), (0,)), ((), ())), preferred_element_type=jnp.float32
    )
    weight_share = fold(fold_pair(weight_term, "core"), NETS)
    weight_share = lax.psum(weight_share, ("z", "xl")).astype(jnp.bfloat16)
    weight_gradient = join_pair(spread(weight_share, NETS), "core")

    net_sum = lax.dot_general(
        block, gathered, (((0,), (0,)), ((), ())), preferred_element_type=jnp.float32
    )
    net_share = fold(fold_pair(fold_pair(net_sum, "core"), "xl"), "z")
    share_rows = net_share.shape[0]
    share_position = lax.axis_index(("core", "xl", "z"))
    pins = lax.dynamic_slice_in_dim(net_pin_count, share_position * share_rows, share_rows)
    grad_share = (net_share / pins.astype(jnp.float32)[:, None]).astype(jnp.bfloat16)
    net_grad = join_pair(join_pair(spread(grad_share, "z"), "xl"), "core")

    cell_part = lax.dot_general(
        block, net_grad, (((1,), (0,)), ((), ())), preferred_element_type=jnp.float32
    )
    cell_total = fold(cell_part, NETS)
    grad_cells = (cell_total / own_root).astype(jnp.bfloat16)
    return (grad_cells, weight_gradient)


def solution(mesh):
    cells, nets = mesh.devices.shape
    fine = Mesh(mesh.devices.reshape(cells // 4, 2, 2, 2, nets // 2), CELLS + NETS)
    every = CELLS + NETS
    in_specs = (
        P(every, None),
        P(every, None),
        P(),
        P(CELLS, NETS, None, None, None),
        P(CELLS, NETS, None, None),
        P(CELLS, NETS),
        P(CELLS),
        P(NETS),
    )
    out_specs = (P(every, None), P())
    return jax.shard_map(shards, mesh=fine, in_specs=in_specs, out_specs=out_specs, check_vma=False)
```

```python
import jax
import jax.numpy as jnp
from jax import lax
from jax.experimental import pallas as pl
from jax.experimental.pallas import tpu as pltpu
from jax.sharding import Mesh
from jax.sharding import PartitionSpec as P

SWAP = ((0, 1), (1, 0))
CELLS = ("z", "xl", "core")
NETS = ("xh", "y")


def dense_kernel(coords_ref, count_ref, tiles_ref, out_ref):
    out_ref[...] = jnp.zeros_like(out_ref)
    slots, tile_len, _ = tiles_ref.shape
    for t in range(slots):

        @pl.when(t < count_ref[0])
        def _():
            row = pl.multiple_of(coords_ref[t, 0] * tile_len, tile_len)
            column = pl.multiple_of(coords_ref[t, 1] * tile_len, tile_len)
            out_ref[pl.ds(row, tile_len), pl.ds(column, tile_len)] = tiles_ref[t]


def dense_block(tiles, coords, count, cells, nets):
    return pl.pallas_call(
        dense_kernel,
        out_shape=jax.ShapeDtypeStruct((cells, nets), tiles.dtype),
        in_specs=[
            pl.BlockSpec(memory_space=pltpu.SMEM),
            pl.BlockSpec(memory_space=pltpu.SMEM),
            pl.BlockSpec(memory_space=pltpu.VMEM),
        ],
        out_specs=pl.BlockSpec(memory_space=pltpu.VMEM),
        compiler_params=pltpu.CompilerParams(vmem_limit_bytes=16 << 20),
        cost_estimate=pl.CostEstimate(flops=0, bytes_accessed=10 << 20, transcendentals=0),
        name="dense_block",
    )(coords, count, tiles)


def half(x, which, dim=0):
    rows = x.shape[dim] // 2
    return lax.dynamic_slice_in_dim(x, which * rows, rows, dim)


def fold_pair(x, axis):
    me = lax.axis_index(axis)
    sent = half(x, 1 - me).astype(jnp.bfloat16)
    return half(x, me) + lax.ppermute(sent, axis, SWAP).astype(jnp.float32)


def join_pair(x, axis):
    return ordered(x, lax.ppermute(x, axis, SWAP), axis)


def ordered(mine, other, axis, dim=0):
    first = lax.axis_index(axis) == 0
    return jnp.concatenate(
        [jnp.where(first, mine, other), jnp.where(first, other, mine)], axis=dim
    )


def copies(x, n):
    return jnp.broadcast_to(x[None], (n,) + x.shape)


def exchange(x, axes):
    return lax.all_to_all(x, axes, 0, 0)


def total(terms):
    return jnp.sum(terms.astype(jnp.float32), axis=0)


def tie(*values):
    return lax.optimization_barrier(values)


def dot(a, b, dims):
    return lax.dot_general(a, b, (dims, ((), ())), preferred_element_type=jnp.float32)


def shards(
    grad_out,
    saved_agg,
    theta,
    tile_values,
    tile_coords,
    block_tile_count,
    cell_degree,
    net_pin_count,
):
    own_rows, features = grad_out.shape
    block_cells = cell_degree.shape[0]
    block_nets = net_pin_count.shape[0]
    part = features // 2
    depth = lax.axis_size("z")
    row_devices = lax.axis_size(NETS)
    net_position = lax.axis_index(NETS)
    own_degree = lax.dynamic_slice_in_dim(cell_degree, net_position * own_rows, own_rows)
    own_root = jnp.sqrt(own_degree.astype(jnp.float32))[:, None]
    share_rows = block_nets // (4 * depth)
    share_position = lax.axis_index(("core", "xl", "z"))
    pins = lax.dynamic_slice_in_dim(net_pin_count, share_position * share_rows, share_rows)
    pins = pins.astype(jnp.float32)[:, None]

    def scaled(i):
        grad_z = dot(grad_out, theta[i * part : (i + 1) * part], ((1,), (1,)))
        return (grad_z / own_root).astype(jnp.bfloat16)

    gathered0 = exchange(copies(scaled(0), row_devices), NETS)
    block = dense_block(
        tile_values[0, 0], tile_coords[0, 0], block_tile_count[0], block_cells, block_nets
    )
    weight = fold_pair(dot(saved_agg, grad_out, ((0,), (0,))), "core").astype(jnp.bfloat16)
    weight_rows = weight.shape[0] // row_devices
    weight = weight.reshape(row_devices, weight_rows, features)
    sent1 = jnp.concatenate(
        [copies(scaled(1), row_devices), weight[:, :, :part], weight[:, :, part:]], axis=1
    )
    sent1, gathered0 = tie(sent1, gathered0)
    gathered1 = exchange(sent1, NETS)

    def net_half(gathered):
        rows = gathered.reshape(block_cells, part)
        return fold_pair(dot(block, rows, ((0,), (0,))), "core")

    quarter0 = fold_pair(net_half(gathered0), "xl").astype(jnp.bfloat16)
    terms0 = quarter0.reshape(depth, share_rows, part)
    gathered1, terms0 = tie(gathered1, terms0)
    summed0 = exchange(terms0, "z")

    weight = total(gathered1[:, own_rows:]).reshape(2, weight_rows, part)
    net1 = net_half(gathered1[:, :own_rows])
    me = lax.axis_index("xl")
    quarter_rows = block_nets // 4
    sent = jnp.concatenate(
        [half(net1, 1 - me), half(weight, 1 - me, 1).reshape(weight_rows, part)], axis=0
    )
    came = lax.ppermute(sent.astype(jnp.bfloat16), "xl", SWAP).astype(jnp.float32)
    quarter1 = half(net1, me) + came[:quarter_rows]
    weight = half(weight, me, 1) + came[quarter_rows:].reshape(2, weight_rows // 2, part)
    lanes = part // 2
    weight = weight.reshape(2, depth, 2, lanes).transpose(1, 0, 2, 3).reshape(depth, 4, lanes)
    quarter1 = quarter1.reshape(depth, share_rows, 2, lanes).transpose(0, 2, 1, 3)
    quarter1 = quarter1.reshape(depth, 2 * share_rows, lanes)
    terms1 = jnp.concatenate([quarter1, weight, jnp.zeros_like(weight)], axis=1)
    summed0, terms1 = tie(summed0, terms1.astype(jnp.bfloat16))
    summed1 = exchange(terms1, "z")

    share0 = (total(summed0) / pins).astype(jnp.bfloat16)
    divisor1 = jnp.concatenate([pins, pins, jnp.ones((8, 1), jnp.float32)], axis=0)
    share1 = (total(summed1) / divisor1).astype(jnp.bfloat16)
    spread1 = exchange(copies(share1, depth), "z")
    sent0, spread1 = tie(copies(share0, depth), spread1)
    spread0 = exchange(sent0, "z")

    quarter1 = spread1[:, : 2 * share_rows].reshape(depth, 2, share_rows, lanes)
    quarter1 = quarter1.transpose(0, 2, 1, 3).reshape(quarter_rows, part)
    weight = spread1[:, 2 * share_rows : 2 * share_rows + 4].reshape(depth, 2, part)
    weight = weight.transpose(1, 0, 2)
    sent = jnp.concatenate([quarter1, weight.reshape(2 * depth, part)], axis=0)
    came = lax.ppermute(sent, "xl", SWAP)
    net1 = ordered(quarter1, came[:quarter_rows], "xl")
    weight = ordered(weight, came[quarter_rows:].reshape(weight.shape), "xl", 1)
    weight = copies(weight.reshape(2 * weight_rows, part), row_devices)

    def cell_terms(net_half_grad):
        net_grad = join_pair(net_half_grad, "core")
        cell_part = dot(block, net_grad, ((1,), (0,))).astype(jnp.bfloat16)
        return cell_part.reshape(row_devices, own_rows, part)

    terms1 = jnp.concatenate([cell_terms(net1), weight], axis=1)
    spread0, terms1 = tie(spread0, terms1)
    cells1 = exchange(terms1, NETS)
    net0 = join_pair(spread0.reshape(quarter_rows, part), "xl")
    cells1, terms0 = tie(cells1, cell_terms(net0))
    cells0 = exchange(terms0, NETS)

    weight = cells1[:, own_rows:].reshape(row_devices, 2, weight_rows, part)
    weight = weight.transpose(0, 2, 1, 3).reshape(row_devices * weight_rows, features)
    weight_gradient = join_pair(weight, "core")
    cell_total = jnp.concatenate([total(cells0), total(cells1[:, :own_rows])], axis=1)
    grad_cells = (cell_total / own_root).astype(jnp.bfloat16)
    return (grad_cells, weight_gradient)


def solution(mesh):
    cells, nets = mesh.devices.shape
    fine = Mesh(mesh.devices.reshape(cells // 4, 2, 2, 2, nets // 2), CELLS + NETS)
    every = CELLS + NETS
    in_specs = (
        P(every, None),
        P(every, None),
        P(),
        P(CELLS, NETS, None, None, None),
        P(CELLS, NETS, None, None),
        P(CELLS, NETS),
        P(CELLS),
        P(NETS),
    )
    out_specs = (P(every, None), P())
    return jax.shard_map(shards, mesh=fine, in_specs=in_specs, out_specs=out_specs, check_vma=False)
```

```python
import jax
import jax.numpy as jnp
from jax import lax
from jax.experimental import pallas as pl
from jax.experimental.pallas import tpu as pltpu
from jax.sharding import Mesh
from jax.sharding import PartitionSpec as P

SWAP = ((0, 1), (1, 0))
CELLS = ("z", "xl", "core")
NETS = ("xh", "y")


def dense_kernel(base_ref, coords_ref, tiles_ref, out_ref):
    blocks, slots, tile_len, _ = tiles_ref.shape
    out_ref[...] = jnp.zeros_like(out_ref)
    for block in range(blocks):
        for t in range(slots):
            row = base_ref[block] + coords_ref[block * slots + t, 0] * tile_len
            column = coords_ref[block * slots + t, 1] * tile_len
            row = pl.multiple_of(row, tile_len)
            column = pl.multiple_of(column, tile_len)
            out_ref[pl.ds(row, tile_len), pl.ds(column, tile_len)] = tiles_ref[block, t]


def dense_blocks(base, coords, tiles, cells, nets):
    size = cells * nets * tiles.dtype.itemsize
    return pl.pallas_call(
        dense_kernel,
        out_shape=jax.ShapeDtypeStruct((cells, nets), tiles.dtype),
        in_specs=[
            pl.BlockSpec(memory_space=pltpu.SMEM),
            pl.BlockSpec(memory_space=pltpu.SMEM),
            pl.BlockSpec(memory_space=pltpu.VMEM),
        ],
        out_specs=pl.BlockSpec(memory_space=pltpu.VMEM),
        compiler_params=pltpu.CompilerParams(vmem_limit_bytes=size + (8 << 20)),
        cost_estimate=pl.CostEstimate(flops=0, bytes_accessed=2 * size, transcendentals=0),
        name="dense_blocks",
    )(base, coords, tiles)


def half(x, which):
    rows = x.shape[0] // 2
    return lax.dynamic_slice_in_dim(x, which * rows, rows)


def swap(x, axis):
    return lax.ppermute(x, axis, SWAP)


def ordered(mine, other, axis, dim=0):
    first = lax.axis_index(axis) == 0
    return jnp.concatenate(
        [jnp.where(first, mine, other), jnp.where(first, other, mine)], axis=dim
    )


def copies(x, n):
    return jnp.broadcast_to(x[None], (n,) + x.shape)


def exchange(x, axes):
    return lax.all_to_all(x, axes, 0, 0)


def total(terms):
    return jnp.sum(terms.astype(jnp.float32), axis=0)


def tie(*values):
    return lax.optimization_barrier(values)


def dot(a, b, dims):
    return lax.dot_general(a, b, (dims, ((), ())), preferred_element_type=jnp.float32)


def shards(
    grad_out,
    saved_agg,
    theta,
    tile_values,
    tile_coords,
    block_tile_count,
    cell_degree,
    net_pin_count,
):
    own_rows, features = grad_out.shape
    block_cells = cell_degree.shape[0]
    block_nets = net_pin_count.shape[0]
    slots = tile_values.shape[2]
    part = features // 2
    lanes = part // 2
    depth = lax.axis_size("z")
    row_devices = lax.axis_size(NETS)
    plane = ("core",) + NETS
    net_position = lax.axis_index(NETS)
    own_degree = lax.dynamic_slice_in_dim(cell_degree, net_position * own_rows, own_rows)
    own_root = jnp.sqrt(own_degree.astype(jnp.float32))[:, None]

    scaled = (dot(grad_out, theta, ((1,), (1,))) / own_root).astype(jnp.bfloat16)
    sent = jnp.concatenate(
        [copies(scaled[:, :part], row_devices), copies(scaled[:, part:], row_devices)], axis=0
    )
    gathered = exchange(sent, plane)

    live = jnp.arange(slots, dtype=jnp.int32) < block_tile_count[0, 0]
    tiles = jnp.where(live[:, None, None], tile_values[0, 0], jnp.zeros((), jnp.bfloat16))
    coords = tile_coords[0, 0]
    tiles = jnp.stack([tiles, swap(tiles, "core")])
    coords = jnp.concatenate([coords, swap(coords, "core")])
    core = lax.axis_index("core")
    base = jnp.stack([core, 1 - core]) * block_cells
    blocks = dense_blocks(base, coords, tiles, 2 * block_cells, block_nets)

    weight = dot(saved_agg, grad_out, ((0,), (0,))).astype(jnp.bfloat16)
    weight_rows = features // row_devices
    weight = jnp.concatenate(
        [
            weight[:, :part].reshape(row_devices, weight_rows, part),
            weight[:, part:].reshape(row_devices, weight_rows, part),
        ],
        axis=0,
    )
    weight, gathered = tie(weight, gathered)
    weight = exchange(weight, plane)

    me = lax.axis_index("xl")
    net_sum = dot(blocks, gathered.reshape(2 * block_cells, part), ((0,), (0,)))
    net_half = half(net_sum, me) + swap(
        half(net_sum, 1 - me).astype(jnp.bfloat16), "xl"
    ).astype(jnp.float32)
    weight, net_half = tie(weight, net_half)
    share_rows = block_nets // (2 * depth)
    few = weight_rows // depth
    net_terms = net_half.reshape(depth, share_rows, 2, lanes).transpose(0, 2, 1, 3)
    weight_terms = total(weight).reshape(depth, few, 2, lanes).transpose(0, 2, 1, 3)
    terms = jnp.concatenate(
        [
            net_terms.reshape(depth, 2 * share_rows, lanes),
            weight_terms.reshape(depth, 2 * few, lanes),
        ],
        axis=1,
    ).astype(jnp.bfloat16)
    share_position = lax.axis_index(("xl", "z"))
    pins = lax.dynamic_slice_in_dim(net_pin_count, share_position * share_rows, share_rows)
    pins = pins.astype(jnp.float32)[:, None]
    divisor = jnp.concatenate([pins, pins, jnp.ones((2 * few, 1), jnp.float32)], axis=0)
    terms, divisor = tie(terms, divisor)
    summed = exchange(terms, "z")
    share = (total(summed) / divisor).astype(jnp.bfloat16)
    mine = exchange(copies(share, depth), "z")
    other = swap(mine, "xl")

    net_rows = 2 * share_rows
    weight = mine[:, net_rows:].astype(jnp.float32) + other[:, net_rows:].astype(jnp.float32)
    weight = weight.astype(jnp.bfloat16).reshape(depth, 2, few, lanes).transpose(0, 2, 1, 3)
    weight = exchange(copies(weight.reshape(weight_rows, part), row_devices), NETS)
    weight = weight.reshape(features, part)

    def unpacked(x):
        x = x[:, :net_rows].reshape(depth, 2, share_rows, lanes).transpose(0, 2, 1, 3)
        return x.reshape(block_nets // 2, part)

    net_grad = ordered(unpacked(mine), unpacked(other), "xl")
    cell_part = dot(blocks, net_grad, ((1,), (0,))).astype(jnp.bfloat16)
    weight, cell_part = tie(weight, cell_part)
    weight_gradient = ordered(weight, swap(weight, "core"), "core", 1)
    terms = exchange(cell_part.reshape(2 * row_devices, own_rows, part), plane)
    cell_total = jnp.concatenate([total(terms[:row_devices]), total(terms[row_devices:])], axis=1)
    grad_cells = (cell_total / own_root).astype(jnp.bfloat16)
    return (grad_cells, weight_gradient)


def solution(mesh):
    cells, nets = mesh.devices.shape
    fine = Mesh(mesh.devices.reshape(cells // 4, 2, 2, 2, nets // 2), CELLS + NETS)
    every = CELLS + NETS
    in_specs = (
        P(every, None),
        P(every, None),
        P(),
        P(CELLS, NETS, None, None, None),
        P(CELLS, NETS, None, None),
        P(CELLS, NETS),
        P(CELLS),
        P(NETS),
    )
    out_specs = (P(every, None), P())
    return jax.shard_map(shards, mesh=fine, in_specs=in_specs, out_specs=out_specs, check_vma=False)
```

```python
import jax
import jax.numpy as jnp
from jax import lax
from jax.experimental import pallas as pl
from jax.experimental.pallas import tpu as pltpu
from jax.sharding import Mesh
from jax.sharding import PartitionSpec as P

SWAP = ((0, 1), (1, 0))
CELLS = ("z", "xl", "core")
NETS = ("xh", "y")
PLANE = ("core",) + NETS
SMEM = pl.BlockSpec(memory_space=pltpu.SMEM)
VMEM = pl.BlockSpec(memory_space=pltpu.VMEM)


def kernel_call(body, name, outs, scratch, flops, nbytes, ins):
    return pl.pallas_call(
        body,
        out_shape=outs,
        in_specs=ins,
        out_specs=jax.tree.map(lambda _: VMEM, outs),
        scratch_shapes=scratch,
        compiler_params=pltpu.CompilerParams(vmem_limit_bytes=40 << 20),
        cost_estimate=pl.CostEstimate(flops=flops, bytes_accessed=nbytes, transcendentals=0),
        name=name,
    )


def mxu(a, b, dims):
    return lax.dot_general(a, b, (dims, ((), ())), preferred_element_type=jnp.float32)


def head_kernel(place_ref, grad_ref, theta_ref, degree_ref, out_ref):
    rows, features = grad_ref.shape
    start = pl.multiple_of(place_ref[0] * rows, rows)
    degree = degree_ref[:, pl.ds(start, rows)].astype(jnp.float32)
    down = lax.broadcasted_iota(jnp.int32, (rows, rows), 0)
    across = lax.broadcasted_iota(jnp.int32, (rows, rows), 1)
    column = jnp.sum(jnp.where(down == across, degree, 0.0), axis=1, keepdims=True)
    grad_z = mxu(grad_ref[...], theta_ref[...], ((1,), (1,)))
    scaled = (grad_z / jnp.sqrt(column)).astype(out_ref.dtype)
    count = out_ref.shape[0] // 2
    part = features // 2
    for i in range(count):
        out_ref[i] = scaled[:, :part]
        out_ref[count + i] = scaled[:, part:]


def flip_kernel(tiles_ref, others_ref, out_ref):
    for block, ref in enumerate((tiles_ref, others_ref)):
        for t in range(ref.shape[0]):
            out_ref[block, t] = ref[t].T


def net_kernel(place_ref, coords_ref, rows_ref, tiles_ref, keep_ref, send_ref, acc):
    blocks, slots, tile_len, _ = tiles_ref.shape
    acc[...] = jnp.zeros_like(acc)
    for block in range(blocks):
        first = (place_ref[1] if block == 0 else 1 - place_ref[1]) * (rows_ref.shape[0] // 2)
        for t in range(slots):
            cell = coords_ref[0, block * slots + t]
            net = pl.multiple_of(coords_ref[1, block * slots + t] * tile_len, tile_len)
            acc[pl.ds(net, tile_len), :] += mxu(
                tiles_ref[block, t], rows_ref[first + cell], ((1,), (0,))
            )
    count = keep_ref.shape[0]
    mine = pl.multiple_of(place_ref[2] * count, count)
    theirs = pl.multiple_of((1 - place_ref[2]) * count, count)
    keep_ref[...] = acc[pl.ds(mine, count), :]
    send_ref[...] = acc[pl.ds(theirs, count), :].astype(send_ref.dtype)


def pack_kernel(keep_ref, came_ref, weight_ref, out_ref):
    depth, _, lanes = out_ref.shape
    rows = keep_ref.shape[0] // depth
    for z in range(depth):
        span = slice(z * rows, (z + 1) * rows)
        summed = keep_ref[span, :] + came_ref[span, :].astype(jnp.float32)
        summed = summed.astype(out_ref.dtype)
        out_ref[z, :rows, :] = summed[:, :lanes]
        out_ref[z, rows : 2 * rows, :] = summed[:, lanes:]
        out_ref[z, 2 * rows :, :] = weight_ref[z]


def cell_kernel(place_ref, coords_ref, mine_ref, other_ref, tiles_ref, others_ref, out_ref, nets, acc):
    depth, _, lanes = mine_ref.shape
    slots, tile_len, _ = tiles_ref.shape
    rows = nets.shape[0] // (2 * depth)
    for block, ref in enumerate((mine_ref, other_ref)):
        first = (place_ref[2] if block == 0 else 1 - place_ref[2]) * (nets.shape[0] // 2)
        for z in range(depth):
            start = pl.multiple_of(first + z * rows, rows)
            nets[pl.ds(start, rows), :lanes] = ref[z, :rows, :]
            nets[pl.ds(start, rows), lanes:] = ref[z, rows : 2 * rows, :]
    acc[...] = jnp.zeros_like(acc)
    for block, ref in enumerate((tiles_ref, others_ref)):
        first = (place_ref[1] if block == 0 else 1 - place_ref[1]) * (acc.shape[0] // 2)
        for t in range(slots):
            cell = coords_ref[0, block * slots + t]
            net = pl.multiple_of(coords_ref[1, block * slots + t] * tile_len, tile_len)
            acc[first + cell] += mxu(ref[t], nets[pl.ds(net, tile_len), :], ((1,), (0,)))
    out_ref[...] = acc[...].astype(out_ref.dtype)


def piece(x, index, count, dim=0):
    size = x.shape[dim] // count
    return lax.dynamic_slice_in_dim(x, index * size, size, dim)


def swap(x, axis):
    return lax.ppermute(x, axis, SWAP)


def ordered(mine, other, axis, dim=0):
    first = lax.axis_index(axis) == 0
    return jnp.concatenate(
        [jnp.where(first, mine, other), jnp.where(first, other, mine)], axis=dim
    )


def fold_pair(x, axis, dim):
    me = lax.axis_index(axis)
    sent = piece(x, 1 - me, 2, dim).astype(jnp.bfloat16)
    return piece(x, me, 2, dim) + swap(sent, axis).astype(jnp.float32)


def turned(x, axis, step):
    size = lax.axis_size(axis)
    return lax.ppermute(x, axis, [(i, (i + step) % size) for i in range(size)])


def fold_ring(x, axis):
    me, size = lax.axis_index(axis), lax.axis_size(axis)
    total = piece(x, me, size)
    for step in range(1, size):
        sent = piece(x, lax.rem(me + step, size), size).astype(jnp.bfloat16)
        total = total + turned(sent, axis, step).astype(jnp.float32)
    return total


def gather_ring(x, axis):
    me, size = lax.axis_index(axis), lax.axis_size(axis)
    every = jnp.stack([x] + [turned(x, axis, step) for step in range(1, size)])
    return jnp.concatenate(
        [
            lax.dynamic_slice_in_dim(every, lax.rem(me - i + size, size), 1)
            for i in range(size)
        ]
    )


def exchange(x, axes):
    return lax.all_to_all(x, axes, 0, 0)


def total(terms):
    return jnp.sum(terms.astype(jnp.float32), axis=0)


def tie(*values):
    return lax.optimization_barrier(values)


def shards(
    grad_out,
    saved_agg,
    theta,
    tile_values,
    tile_coords,
    block_tile_count,
    cell_degree,
    net_pin_count,
):
    own_rows, features = grad_out.shape
    block_cells = cell_degree.shape[0]
    block_nets = net_pin_count.shape[0]
    slots, tile_len = tile_values.shape[2], tile_values.shape[3]
    part = features // 2
    lanes = part // 2
    depth = lax.axis_size("z")
    row_devices = lax.axis_size(NETS)
    share_rows = block_nets // (2 * depth)
    net_rows = 2 * share_rows
    weight_rows = features // row_devices
    few = weight_rows // depth
    shape = jax.ShapeDtypeStruct
    narrow, wide = jnp.bfloat16, jnp.float32
    net_position = lax.axis_index(NETS)
    place = jnp.stack([net_position, lax.axis_index("core"), lax.axis_index("xl")])

    sent = kernel_call(
        head_kernel,
        "head",
        shape((2 * row_devices, own_rows, part), narrow),
        [],
        2 * own_rows * features * features,
        4 << 20,
        [SMEM, VMEM, VMEM, VMEM],
    )(place, grad_out, theta, cell_degree.reshape(1, block_cells))

    tile_values, tile_coords, saved_agg, sent = tie(tile_values, tile_coords, saved_agg, sent)
    gathered = exchange(sent, PLANE)
    live = jnp.arange(slots, dtype=jnp.int32) < block_tile_count[0, 0]
    tiles = jnp.where(live[:, None, None], tile_values[0, 0], jnp.zeros((), narrow))
    coords = tile_coords[0, 0].T
    others = swap(tiles, "core")
    coords = jnp.concatenate([coords, swap(coords, "core")], axis=1)
    weight = mxu(saved_agg, grad_out, ((0,), (0,)))
    weight = fold_pair(weight, "core", 1)
    weight = fold_ring(fold_pair(weight, "xh", 0), "y")
    weight = weight.astype(narrow).reshape(depth, few, 2, lanes).transpose(0, 2, 1, 3)
    weight = weight.reshape(depth, 2 * few, lanes)
    flipped = kernel_call(
        flip_kernel,
        "flip",
        shape((2,) + tiles.shape, narrow),
        [],
        0,
        2 << 20,
        [VMEM, VMEM],
    )(tiles, others)
    share_position = lax.axis_index(("xl", "z"))
    pins = lax.dynamic_slice_in_dim(net_pin_count, share_position * share_rows, share_rows)
    pins = pins.astype(wide)[:, None]
    divisor = jnp.concatenate([pins, pins, jnp.ones((2 * few, 1), wide)], axis=0)
    own_degree = lax.dynamic_slice_in_dim(cell_degree, net_position * own_rows, own_rows)
    own_root = jnp.sqrt(own_degree.astype(wide))[:, None]
    gathered, weight, flipped, coords, divisor, own_root = tie(
        gathered, weight, flipped, coords, divisor, own_root
    )

    keep, sent = kernel_call(
        net_kernel,
        "net_sums",
        (shape((block_nets // 2, part), wide), shape((block_nets // 2, part), narrow)),
        [pltpu.VMEM((block_nets, part), wide)],
        4 * slots * tile_len * tile_len * part,
        5 << 20,
        [SMEM, SMEM, VMEM, VMEM],
    )(place, coords, gathered.reshape(-1, tile_len, part), flipped)
    terms = kernel_call(
        pack_kernel,
        "pack",
        shape((depth, net_rows + 2 * few, lanes), narrow),
        [],
        0,
        1 << 20,
        [VMEM, VMEM, VMEM],
    )(keep, swap(sent, "xl"), weight)
    summed = exchange(terms, "z")
    share = (total(summed) / divisor).astype(narrow)
    mine = exchange(jnp.broadcast_to(share[None], terms.shape), "z")
    other = swap(mine, "xl")
    cell_terms = kernel_call(
        cell_kernel,
        "cell_terms",
        shape((2 * block_cells // tile_len, tile_len, part), narrow),
        [
            pltpu.VMEM((block_nets, part), narrow),
            pltpu.VMEM((2 * block_cells // tile_len, tile_len, part), wide),
        ],
        4 * slots * tile_len * tile_len * part,
        4 << 20,
        [SMEM, SMEM, VMEM, VMEM, VMEM, VMEM],
    )(place, coords, mine, other, tiles, others)
    cells = exchange(cell_terms.reshape(2 * row_devices, own_rows, part), PLANE)

    weight = mine[:, net_rows:].astype(wide) + other[:, net_rows:].astype(wide)
    weight, cell_terms = tie(weight.astype(narrow), cell_terms)
    weight = weight.reshape(depth, 2, few, lanes).transpose(0, 2, 1, 3)
    weight = weight.reshape(1, weight_rows, part)
    weight = gather_ring(ordered(weight, swap(weight, "xh"), "xh"), "y")
    weight = weight.transpose(1, 0, 2, 3).reshape(features, part)
    weight_gradient = ordered(weight, swap(weight, "core"), "core", 1)

    cell_total = jnp.concatenate([total(cells[:row_devices]), total(cells[row_devices:])], axis=1)
    grad_cells = (cell_total / own_root).astype(narrow)
    return (grad_cells, weight_gradient)


def solution(mesh):
    cells, nets = mesh.devices.shape
    fine = Mesh(mesh.devices.reshape(cells // 4, 2, 2, 2, nets // 2), CELLS + NETS)
    every = CELLS + NETS
    in_specs = (
        P(every, None),
        P(every, None),
        P(),
        P(CELLS, NETS, None, None, None),
        P(CELLS, NETS, None, None),
        P(CELLS, NETS),
        P(CELLS),
        P(NETS),
    )
    out_specs = (P(every, None), P())
    return jax.shard_map(shards, mesh=fine, in_specs=in_specs, out_specs=out_specs, check_vma=False)
```

```python
import jax
import jax.numpy as jnp
from jax import lax
from jax.experimental import pallas as pl
from jax.experimental.pallas import tpu as pltpu
from jax.sharding import Mesh
from jax.sharding import PartitionSpec as P

SWAP = ((0, 1), (1, 0))
CELLS = ("z", "xl", "core")
NETS = ("xh", "y")
PLANE = ("core",) + NETS
SMEM = pl.BlockSpec(memory_space=pltpu.SMEM)
VMEM = pl.BlockSpec(memory_space=pltpu.VMEM)
HBM = pl.BlockSpec(memory_space=pltpu.HBM)


def kernel_call(body, name, outs, scratch, flops, nbytes, ins, **grid):
    return pl.pallas_call(
        body,
        out_shape=outs,
        in_specs=ins,
        scratch_shapes=scratch,
        compiler_params=pltpu.CompilerParams(vmem_limit_bytes=grid.pop("vmem", 40) << 20),
        cost_estimate=pl.CostEstimate(flops=flops, bytes_accessed=nbytes, transcendentals=0),
        name=name,
        **({"out_specs": jax.tree.map(lambda _: VMEM, outs)} | grid),
    )


def mxu(a, b, dims):
    return lax.dot_general(a, b, (dims, ((), ())), preferred_element_type=jnp.float32)


def head_kernel(
    place_ref,
    grad_hbm,
    theta_hbm,
    saved_hbm,
    degree_hbm,
    out_hbm,
    grad_ref,
    theta_ref,
    saved_ref,
    degree_ref,
    scaled_ref,
    weight_ref,
    in_sems,
    out_sems,
):
    rows, features = grad_ref.shape
    count, part = out_hbm.shape[0] // 2, features // 2
    share = out_hbm.shape[1] - rows
    loads = [
        pltpu.make_async_copy(source, target, in_sems.at[i])
        for i, (source, target) in enumerate(
            (
                (degree_hbm, degree_ref),
                (grad_hbm, grad_ref),
                (theta_hbm, theta_ref),
                (saved_hbm, saved_ref),
            )
        )
    ]
    for load in loads:
        load.start()
    loads[0].wait()
    start = pl.multiple_of(place_ref[0] * rows, rows)
    degree = degree_ref[:, pl.ds(start, rows)].astype(jnp.float32)
    down = lax.broadcasted_iota(jnp.int32, (rows, rows), 0)
    across = lax.broadcasted_iota(jnp.int32, (rows, rows), 1)
    column = jnp.sum(jnp.where(down == across, degree, 0.0), axis=1, keepdims=True)
    root = jnp.sqrt(column)
    loads[1].wait()
    loads[2].wait()
    stores = []

    def store(source, i, first, size, kind):
        stores.append(
            pltpu.make_async_copy(
                source, out_hbm.at[i, pl.ds(first, size), :], out_sems.at[kind, i]
            )
        )
        stores[-1].start()

    for half in range(2):
        grad_z = mxu(grad_ref[...], theta_ref[half * part : (half + 1) * part, :], ((1,), (1,)))
        scaled_ref[half] = (grad_z / root).astype(scaled_ref.dtype)
        for i in range(count):
            store(scaled_ref.at[half], half * count + i, 0, rows, 0)
    loads[3].wait()
    for half in range(2):
        terms = mxu(saved_ref[...], grad_ref[:, half * part : (half + 1) * part], ((0,), (0,)))
        weight_ref[half] = terms.astype(weight_ref.dtype)
        for i in range(count):
            source = weight_ref.at[half, pl.ds(i * share, share), :]
            store(source, half * count + i, rows, share, 1)
    for copy in stores:
        copy.wait()


def net_kernel(
    place_ref, coords_ref, rows_ref, tiles_ref, others_ref, keep_ref, send_ref, weight_ref, acc
):
    slots, tile_len, _ = tiles_ref.shape
    devices, lines, _ = rows_ref.shape
    depth, few, lanes = weight_ref.shape
    own_rows = lines - depth * few // 2
    per_device = own_rows // tile_len
    acc[...] = jnp.zeros_like(acc)
    for block, ref in enumerate((tiles_ref, others_ref)):
        first = (place_ref[1] if block == 0 else 1 - place_ref[1]) * (devices // 2)
        for t in range(slots):
            cell = coords_ref[0, block * slots + t]
            net = pl.multiple_of(coords_ref[1, block * slots + t] * tile_len, tile_len)
            row = pl.multiple_of(lax.rem(cell, per_device) * tile_len, tile_len)
            cells = rows_ref[first + lax.div(cell, per_device), pl.ds(row, tile_len), :]
            acc[pl.ds(net, tile_len), :] += mxu(ref[t].T, cells, ((1,), (0,)))
    count = keep_ref.shape[0]
    mine = pl.multiple_of(place_ref[2] * count, count)
    theirs = pl.multiple_of((1 - place_ref[2]) * count, count)
    keep_ref[...] = acc[pl.ds(mine, count), :]
    send_ref[...] = acc[pl.ds(theirs, count), :].astype(send_ref.dtype)
    weight = rows_ref[0, own_rows:, :].astype(jnp.float32)
    for i in range(1, devices):
        weight = weight + rows_ref[i, own_rows:, :].astype(jnp.float32)
    runs = depth // 2
    for z in range(depth):
        line, lane = z % runs * few, z // runs * lanes
        weight_ref[z] = weight[line : line + few, lane : lane + lanes].astype(weight_ref.dtype)


def pack_kernel(keep_ref, came_ref, weight_ref, out_ref):
    depth, _, lanes = out_ref.shape
    rows = keep_ref.shape[0] // depth
    for z in range(depth):
        span = slice(z * rows, (z + 1) * rows)
        summed = keep_ref[span, :] + came_ref[span, :].astype(jnp.float32)
        summed = summed.astype(out_ref.dtype)
        out_ref[z, :rows, :] = summed[:, :lanes]
        out_ref[z, rows : 2 * rows, :] = summed[:, lanes:]
        out_ref[z, 2 * rows :, :] = weight_ref[z]


def cell_kernel(
    place_ref, coords_ref, mine_ref, other_ref, tiles_ref, others_ref, out_hbm, nets, acc, out_ref, sems
):
    depth, lines, lanes = mine_ref.shape
    slots, tile_len, _ = tiles_ref.shape
    rows = nets.shape[0] // (2 * depth)
    for block, ref in enumerate((mine_ref, other_ref)):
        first = (place_ref[2] if block == 0 else 1 - place_ref[2]) * (nets.shape[0] // 2)
        for z in range(depth):
            start = pl.multiple_of(first + z * rows, rows)
            nets[pl.ds(start, rows), :lanes] = ref[z, :rows, :]
            nets[pl.ds(start, rows), lanes:] = ref[z, rows : 2 * rows, :]
    devices = out_ref.shape[0]
    count = devices // 2
    per_device = acc.shape[0] // count
    few, runs = lines - 2 * rows, depth // 2
    for z in range(depth):
        summed = mine_ref[z, 2 * rows :, :].astype(jnp.float32)
        summed = summed + other_ref[z, 2 * rows :, :].astype(jnp.float32)
        summed = summed.astype(out_ref.dtype)
        line, lane = per_device * tile_len + z % runs * few, z // runs * lanes
        for i in range(devices):
            out_ref[i, line : line + few, lane : lane + lanes] = summed
    copies = []
    for block, ref in enumerate((tiles_ref, others_ref)):
        first = (place_ref[1] if block == 0 else 1 - place_ref[1]) * count
        acc[...] = jnp.zeros_like(acc)
        for t in range(slots):
            cell = coords_ref[0, block * slots + t]
            net = pl.multiple_of(coords_ref[1, block * slots + t] * tile_len, tile_len)
            acc[cell] += mxu(ref[t], nets[pl.ds(net, tile_len), :], ((1,), (0,)))
        for i in range(count):
            at = block * count + i
            for j in range(per_device):
                span = slice(j * tile_len, (j + 1) * tile_len)
                out_ref[at, span, :] = acc[i * per_device + j].astype(out_ref.dtype)
            copies.append(
                pltpu.make_async_copy(out_ref.at[at], out_hbm.at[first + i], sems.at[at])
            )
            copies[-1].start()
    for copy in copies:
        copy.wait()


def tail_kernel(terms_ref, root_ref, cells_ref, weight_ref):
    devices, lines, part = terms_ref.shape
    rows, features = cells_ref.shape
    count = devices // 2
    share = lines - rows
    for half in range(2):
        span = slice(half * part, (half + 1) * part)
        total = terms_ref[half * count, :rows, :].astype(jnp.float32)
        for i in range(1, count):
            total = total + terms_ref[half * count + i, :rows, :].astype(jnp.float32)
        cells_ref[:, span] = (total / root_ref[...]).astype(cells_ref.dtype)
        for i in range(count):
            weight_ref[i * share : (i + 1) * share, span] = terms_ref[half * count + i, rows:, :]


def swap(x, axis):
    return lax.ppermute(x, axis, SWAP)


def exchange(x, axes):
    return lax.all_to_all(x, axes, 0, 0)


def tie(*values):
    return lax.optimization_barrier(values)


def shards(
    grad_out,
    saved_agg,
    theta,
    tile_values,
    tile_coords,
    block_tile_count,
    cell_degree,
    net_pin_count,
):
    own_rows, features = grad_out.shape
    block_cells = cell_degree.shape[0]
    block_nets = net_pin_count.shape[0]
    slots, tile_len = tile_values.shape[2], tile_values.shape[3]
    part = features // 2
    lanes = part // 2
    depth = lax.axis_size("z")
    row_devices = lax.axis_size(NETS)
    share_rows = block_nets // (2 * depth)
    net_rows = 2 * share_rows
    weight_rows = features // row_devices
    few = 2 * weight_rows // depth
    lines = own_rows + weight_rows
    shape = jax.ShapeDtypeStruct
    narrow, wide = jnp.bfloat16, jnp.float32
    net_position = lax.axis_index(NETS)
    place = jnp.stack([net_position, lax.axis_index("core"), lax.axis_index("xl")])

    sent = kernel_call(
        head_kernel,
        "head",
        shape((2 * row_devices, lines, part), narrow),
        [
            pltpu.VMEM((own_rows, features), narrow),
            pltpu.VMEM((features, features), narrow),
            pltpu.VMEM((own_rows, features), narrow),
            pltpu.VMEM((1, block_cells), jnp.int32),
            pltpu.VMEM((2, own_rows, part), narrow),
            pltpu.VMEM((2, features, part), narrow),
            pltpu.SemaphoreType.DMA((4,)),
            pltpu.SemaphoreType.DMA((2, 2 * row_devices)),
        ],
        4 * own_rows * features * features,
        4 << 20,
        [SMEM, HBM, HBM, HBM, HBM],
        out_specs=HBM,
        vmem=60,
    )(place, grad_out, theta, saved_agg, cell_degree.reshape(1, block_cells))
    tile_values, tile_coords, sent = tie(tile_values, tile_coords, sent)
    gathered = exchange(sent, PLANE)

    live = jnp.arange(slots, dtype=jnp.int32) < block_tile_count[0, 0]
    tiles = jnp.where(live[:, None, None], tile_values[0, 0], jnp.zeros((), narrow))
    coords = tile_coords[0, 0].T
    others = swap(tiles, "core")
    coords = jnp.concatenate([coords, swap(coords, "core")], axis=1)
    share_position = lax.axis_index(("xl", "z"))
    pins = lax.dynamic_slice_in_dim(net_pin_count, share_position * share_rows, share_rows)
    pins = pins.astype(wide)[:, None]
    divisor = jnp.concatenate([pins, pins, jnp.ones((few, 1), wide)], axis=0)
    own_degree = lax.dynamic_slice_in_dim(cell_degree, net_position * own_rows, own_rows)
    own_root = jnp.sqrt(own_degree.astype(wide))[:, None]
    gathered, tiles, others, coords, divisor, own_root = tie(
        gathered, tiles, others, coords, divisor, own_root
    )

    keep, sent, weight = kernel_call(
        net_kernel,
        "net_sums",
        (
            shape((block_nets // 2, part), wide),
            shape((block_nets // 2, part), narrow),
            shape((depth, few, lanes), narrow),
        ),
        [pltpu.VMEM((block_nets, part), wide)],
        4 * slots * tile_len * tile_len * part,
        5 << 20,
        [SMEM, SMEM, VMEM, VMEM, VMEM],
    )(place, coords, gathered, tiles, others)
    terms = kernel_call(
        pack_kernel,
        "pack",
        shape((depth, net_rows + few, lanes), narrow),
        [],
        0,
        1 << 20,
        [VMEM, VMEM, VMEM],
    )(keep, swap(sent, "xl"), weight)
    summed = jnp.sum(exchange(terms, "z").astype(wide), axis=0)
    share = (summed / divisor).astype(narrow)
    mine = exchange(jnp.broadcast_to(share[None], terms.shape), "z")
    other = swap(mine, "xl")
    cell_terms = kernel_call(
        cell_kernel,
        "cell_terms",
        shape((2 * row_devices, lines, part), narrow),
        [
            pltpu.VMEM((block_nets, part), narrow),
            pltpu.VMEM((block_cells // tile_len, tile_len, part), wide),
            pltpu.VMEM((2 * row_devices, lines, part), narrow),
            pltpu.SemaphoreType.DMA((2 * row_devices,)),
        ],
        4 * slots * tile_len * tile_len * part,
        4 << 20,
        [SMEM, SMEM, VMEM, VMEM, VMEM, VMEM],
        out_specs=HBM,
        vmem=60,
    )(place, coords, mine, other, tiles, others)
    return kernel_call(
        tail_kernel,
        "tail",
        (shape(grad_out.shape, narrow), shape((features, features), narrow)),
        [],
        0,
        4 << 20,
        [VMEM, VMEM],
    )(exchange(cell_terms, PLANE), own_root)


def solution(mesh):
    cells, nets = mesh.devices.shape
    fine = Mesh(mesh.devices.reshape(cells // 4, 2, 2, 2, nets // 2), CELLS + NETS)
    every = CELLS + NETS
    in_specs = (
        P(every, None),
        P(every, None),
        P(),
        P(CELLS, NETS, None, None, None),
        P(CELLS, NETS, None, None),
        P(CELLS, NETS),
        P(CELLS),
        P(NETS),
    )
    out_specs = (P(every, None), P())
    return jax.shard_map(shards, mesh=fine, in_specs=in_specs, out_specs=out_specs, check_vma=False)
```

```python
import jax
import jax.numpy as jnp
from jax import lax
from jax.experimental import pallas as pl
from jax.experimental.pallas import tpu as pltpu
from jax.sharding import Mesh
from jax.sharding import PartitionSpec as P

SWAP = ((0, 1), (1, 0))
CELLS = ("z", "xl", "core")
NETS = ("xh", "y")
PLANE = ("core",) + NETS
SMEM = pl.BlockSpec(memory_space=pltpu.SMEM)
VMEM = pl.BlockSpec(memory_space=pltpu.VMEM)
HBM = pl.BlockSpec(memory_space=pltpu.HBM)


def kernel_call(body, name, outs, scratch, flops, nbytes, ins, **grid):
    return pl.pallas_call(
        body,
        out_shape=outs,
        in_specs=ins,
        scratch_shapes=scratch,
        compiler_params=pltpu.CompilerParams(vmem_limit_bytes=grid.pop("vmem", 40) << 20),
        cost_estimate=pl.CostEstimate(flops=flops, bytes_accessed=nbytes, transcendentals=0),
        name=name,
        **({"out_specs": jax.tree.map(lambda _: VMEM, outs)} | grid),
    )


def mxu(a, b, dims):
    return lax.dot_general(a, b, (dims, ((), ())), preferred_element_type=jnp.float32)


def head_kernel(
    place_ref,
    grad_hbm,
    theta_hbm,
    saved_hbm,
    degree_hbm,
    out_hbm,
    grad_ref,
    theta_ref,
    saved_ref,
    degree_ref,
    scaled_ref,
    weight_ref,
    in_sems,
    out_sems,
):
    rows, features = grad_ref.shape
    parts, _, part = scaled_ref.shape
    devices, weight_lines, _ = weight_ref.shape
    count, share = devices // parts, weight_lines // parts
    loads = [
        pltpu.make_async_copy(source, target, in_sems.at[i])
        for i, (source, target) in enumerate(
            (
                (degree_hbm, degree_ref),
                (grad_hbm, grad_ref),
                (theta_hbm, theta_ref),
                (saved_hbm, saved_ref),
            )
        )
    ]
    for load in loads:
        load.start()
    loads[0].wait()
    start = pl.multiple_of(place_ref[0] * rows, rows)
    degree = degree_ref[:, pl.ds(start, rows)].astype(jnp.float32)
    down = lax.broadcasted_iota(jnp.int32, (rows, rows), 0)
    across = lax.broadcasted_iota(jnp.int32, (rows, rows), 1)
    column = jnp.sum(jnp.where(down == across, degree, 0.0), axis=1, keepdims=True)
    root = jnp.sqrt(column)
    loads[1].wait()
    loads[2].wait()
    stores = []

    def store(source, i, first, size, kind):
        stores.append(
            pltpu.make_async_copy(
                source, out_hbm.at[i, pl.ds(first, size), :], out_sems.at[kind, i]
            )
        )
        stores[-1].start()

    scaled = (mxu(grad_ref[...], theta_ref[...], ((1,), (1,))) / root).astype(scaled_ref.dtype)
    for q in range(parts):
        scaled_ref[q] = scaled[:, q * part : (q + 1) * part]
        for i in range(count):
            store(scaled_ref.at[q], q * count + i, 0, rows, 0)
    loads[3].wait()
    terms = mxu(saved_ref[...], grad_ref[...], ((0,), (0,))).astype(weight_ref.dtype)
    for i in range(devices):
        for q in range(parts):
            weight_ref[i, q * share : (q + 1) * share, :] = terms[
                i * share : (i + 1) * share, q * part : (q + 1) * part
            ]
        store(weight_ref.at[i], i, rows, weight_lines, 1)
    for copy in stores:
        copy.wait()


def sides(place_ref, block):
    core = place_ref[1] if block < 2 else 1 - place_ref[1]
    high = place_ref[3] if block % 2 == 0 else 1 - place_ref[3]
    return core, high


def net_kernel(
    place_ref, coords_ref, rows_ref, tiles_ref, keep_ref, send_ref, weight_ref, acc
):
    blocks, slots, tile_len, _ = tiles_ref.shape
    devices, lines, _ = rows_ref.shape
    depth, few, _ = weight_ref.shape
    own_rows = lines - depth * few
    per_device = own_rows // tile_len
    count = keep_ref.shape[0]
    acc[...] = jnp.zeros_like(acc)
    for block in range(blocks):
        core, high = sides(place_ref, block)
        for t in range(slots):
            cell = coords_ref[0, block * slots + t]
            net = high * count + coords_ref[1, block * slots + t] * tile_len
            net = pl.multiple_of(net, tile_len)
            row = pl.multiple_of(lax.rem(cell, per_device) * tile_len, tile_len)
            source = core * (devices // 2) + lax.div(cell, per_device)
            cells = rows_ref[source, pl.ds(row, tile_len), :]
            acc[pl.ds(net, tile_len), :] += mxu(tiles_ref[block, t].T, cells, ((1,), (0,)))
    mine = pl.multiple_of(place_ref[2] * count, count)
    theirs = pl.multiple_of((1 - place_ref[2]) * count, count)
    keep_ref[...] = acc[pl.ds(mine, count), :]
    send_ref[...] = acc[pl.ds(theirs, count), :].astype(send_ref.dtype)
    weight = rows_ref[0, own_rows:, :].astype(jnp.float32)
    for i in range(1, devices):
        weight = weight + rows_ref[i, own_rows:, :].astype(jnp.float32)
    for z in range(depth):
        weight_ref[z] = weight[z * few : (z + 1) * few].astype(weight_ref.dtype)


def pack_kernel(keep_ref, came_ref, weight_ref, out_ref):
    depth = out_ref.shape[0]
    rows = keep_ref.shape[0] // depth
    for z in range(depth):
        span = slice(z * rows, (z + 1) * rows)
        summed = keep_ref[span, :] + came_ref[span, :].astype(jnp.float32)
        out_ref[z, :rows, :] = summed.astype(out_ref.dtype)
        out_ref[z, rows:, :] = weight_ref[z]


def cell_kernel(
    place_ref, coords_ref, mine_ref, other_ref, tiles_ref, out_hbm, nets, acc, out_ref, sems
):
    depth, lines, _ = mine_ref.shape
    blocks, slots, tile_len, _ = tiles_ref.shape
    block_nets = nets.shape[0] // 2
    rows = block_nets // depth
    for side, ref in enumerate((mine_ref, other_ref)):
        first = (place_ref[2] if side == 0 else 1 - place_ref[2]) * block_nets
        for z in range(depth):
            start = pl.multiple_of(first + z * rows, rows)
            nets[pl.ds(start, rows), :] = ref[z, :rows, :]
    devices = out_ref.shape[0]
    count = devices // 2
    per_device = acc.shape[0] // count
    few = lines - rows
    for z in range(depth):
        summed = mine_ref[z, rows:, :].astype(jnp.float32)
        summed = (summed + other_ref[z, rows:, :].astype(jnp.float32)).astype(out_ref.dtype)
        line = per_device * tile_len + z * few
        for i in range(devices):
            out_ref[i, line : line + few, :] = summed
    copies = []
    for side in range(2):
        acc[...] = jnp.zeros_like(acc)
        for block in range(side * 2, side * 2 + 2):
            core, high = sides(place_ref, block)
            for t in range(slots):
                cell = coords_ref[0, block * slots + t]
                net = high * block_nets + coords_ref[1, block * slots + t] * tile_len
                net = pl.multiple_of(net, tile_len)
                acc[cell] += mxu(
                    tiles_ref[block, t], nets[pl.ds(net, tile_len), :], ((1,), (0,))
                )
        for i in range(count):
            at = side * count + i
            for j in range(per_device):
                span = slice(j * tile_len, (j + 1) * tile_len)
                out_ref[at, span, :] = acc[i * per_device + j].astype(out_ref.dtype)
            copies.append(
                pltpu.make_async_copy(out_ref.at[at], out_hbm.at[core * count + i], sems.at[at])
            )
            copies[-1].start()
    for copy in copies:
        copy.wait()


def tail_kernel(terms_ref, root_ref, cells_ref, weight_ref):
    devices, lines, part = terms_ref.shape
    rows, features = cells_ref.shape
    parts = features // part
    count, share = devices // parts, (lines - rows) // parts
    for q in range(parts):
        span = slice(q * part, (q + 1) * part)
        total = terms_ref[q * count, :rows, :].astype(jnp.float32)
        for i in range(1, count):
            total = total + terms_ref[q * count + i, :rows, :].astype(jnp.float32)
        cells_ref[:, span] = (total / root_ref[...]).astype(cells_ref.dtype)
        for i in range(devices):
            first = rows + q * share
            weight_ref[i * share : (i + 1) * share, span] = terms_ref[i, first : first + share, :]


def swap(x, axis):
    return lax.ppermute(x, axis, SWAP)


def exchange(x, axes):
    return lax.all_to_all(x, axes, 0, 0)


def tie(*values):
    return lax.optimization_barrier(values)


def shards(
    grad_out,
    saved_agg,
    theta,
    tile_values,
    tile_coords,
    block_tile_count,
    cell_degree,
    net_pin_count,
):
    own_rows, features = grad_out.shape
    block_cells = cell_degree.shape[0]
    block_nets = net_pin_count.shape[0]
    slots, tile_len = tile_values.shape[2], tile_values.shape[3]
    parts = 4
    part = features // parts
    depth = lax.axis_size("z")
    devices = lax.axis_size(PLANE)
    share_rows = block_nets // depth
    weight_lines = features // devices * parts
    few = weight_lines // depth
    lines = own_rows + weight_lines
    shape = jax.ShapeDtypeStruct
    narrow, wide = jnp.bfloat16, jnp.float32
    net_position = lax.axis_index(NETS)
    low, high = lax.axis_index("xl"), lax.axis_index("xh")
    place = jnp.stack([net_position, lax.axis_index("core"), low, high])

    tiles = tile_values[0]
    tiles = jnp.concatenate([tiles, swap(tiles, "xh")])
    guide = jnp.concatenate(
        [
            tile_coords[0, 0].T.reshape(-1),
            jnp.broadcast_to(block_tile_count[0], (slots,)),
            net_pin_count,
        ]
    )
    guide_other = swap(guide, "xh")
    sent = kernel_call(
        head_kernel,
        "head",
        shape((devices, lines, part), narrow),
        [
            pltpu.VMEM((own_rows, features), narrow),
            pltpu.VMEM((features, features), narrow),
            pltpu.VMEM((own_rows, features), narrow),
            pltpu.VMEM((1, block_cells), jnp.int32),
            pltpu.VMEM((parts, own_rows, part), narrow),
            pltpu.VMEM((devices, weight_lines, part), narrow),
            pltpu.SemaphoreType.DMA((4,)),
            pltpu.SemaphoreType.DMA((2, devices)),
        ],
        4 * own_rows * features * features,
        4 << 20,
        [SMEM, HBM, HBM, HBM, HBM],
        out_specs=HBM,
        vmem=60,
    )(place, grad_out, theta, saved_agg, cell_degree.reshape(1, block_cells))
    guide, sent = tie(guide, sent)
    gathered = exchange(sent, PLANE)

    coords = jnp.stack([guide[: 3 * slots], guide_other[: 3 * slots]])
    coords = jnp.concatenate([coords, swap(coords, "core")])
    coords = coords.reshape(4, 3, slots).transpose(1, 0, 2).reshape(3, 4 * slots)
    tiles = jnp.concatenate([tiles, swap(tiles, "core")])
    live = jnp.arange(slots, dtype=jnp.int32) < coords[2].reshape(4, slots)
    tiles = jnp.where(live[:, :, None, None], tiles, jnp.zeros((), narrow))
    pins = jnp.where(low == high, guide, guide_other)[3 * slots :]
    pins = pins.astype(wide).reshape(depth, share_rows)
    pins = lax.dynamic_index_in_dim(pins, lax.axis_index("z"), 0, False)[:, None]
    divisor = jnp.concatenate([pins, jnp.ones((few, 1), wide)], axis=0)
    own_degree = lax.dynamic_slice_in_dim(cell_degree, net_position * own_rows, own_rows)
    own_root = jnp.sqrt(own_degree.astype(wide))[:, None]
    gathered, tiles, coords, divisor, own_root = tie(gathered, tiles, coords, divisor, own_root)

    keep, sent, weight = kernel_call(
        net_kernel,
        "net_sums",
        (
            shape((block_nets, part), wide),
            shape((block_nets, part), narrow),
            shape((depth, few, part), narrow),
        ),
        [pltpu.VMEM((2 * block_nets, part), wide)],
        8 * slots * tile_len * tile_len * part,
        5 << 20,
        [SMEM, SMEM, VMEM, VMEM],
    )(place, coords, gathered, tiles)
    terms = kernel_call(
        pack_kernel,
        "pack",
        shape((depth, share_rows + few, part), narrow),
        [],
        0,
        1 << 20,
        [VMEM, VMEM, VMEM],
    )(keep, swap(sent, "xl"), weight)
    summed = jnp.sum(exchange(terms, "z").astype(wide), axis=0)
    share = (summed / divisor).astype(narrow)
    mine = exchange(jnp.broadcast_to(share[None], terms.shape), "z")
    other = swap(mine, "xl")
    cell_terms = kernel_call(
        cell_kernel,
        "cell_terms",
        shape((devices, lines, part), narrow),
        [
            pltpu.VMEM((2 * block_nets, part), narrow),
            pltpu.VMEM((block_cells // tile_len, tile_len, part), wide),
            pltpu.VMEM((devices, lines, part), narrow),
            pltpu.SemaphoreType.DMA((devices,)),
        ],
        8 * slots * tile_len * tile_len * part,
        4 << 20,
        [SMEM, SMEM, VMEM, VMEM, VMEM],
        out_specs=HBM,
        vmem=60,
    )(place, coords, mine, other, tiles)
    return kernel_call(
        tail_kernel,
        "tail",
        (shape(grad_out.shape, narrow), shape((features, features), narrow)),
        [],
        0,
        4 << 20,
        [VMEM, VMEM],
    )(exchange(cell_terms, PLANE), own_root)


def solution(mesh):
    cells, nets = mesh.devices.shape
    fine = Mesh(mesh.devices.reshape(cells // 4, 2, 2, 2, nets // 2), CELLS + NETS)
    every = CELLS + NETS
    in_specs = (
        P(every, None),
        P(every, None),
        P(),
        P(CELLS, NETS, None, None, None),
        P(CELLS, NETS, None, None),
        P(CELLS, NETS),
        P(CELLS),
        P(NETS),
    )
    out_specs = (P(every, None), P())
    return jax.shard_map(shards, mesh=fine, in_specs=in_specs, out_specs=out_specs, check_vma=False)
```

```python
import jax
import jax.numpy as jnp
from jax import lax
from jax.experimental import pallas as pl
from jax.experimental.pallas import tpu as pltpu
from jax.sharding import Mesh
from jax.sharding import PartitionSpec as P

SWAP = ((0, 1), (1, 0))
CELLS = ("z", "xl", "core")
NETS = ("xh", "y")
PLANE = ("core",) + NETS
SMEM = pl.BlockSpec(memory_space=pltpu.SMEM)
VMEM = pl.BlockSpec(memory_space=pltpu.VMEM)
HBM = pl.BlockSpec(memory_space=pltpu.HBM)


def kernel_call(body, name, outs, scratch, flops, nbytes, ins, **grid):
    return pl.pallas_call(
        body,
        out_shape=outs,
        in_specs=ins,
        scratch_shapes=scratch,
        compiler_params=pltpu.CompilerParams(vmem_limit_bytes=grid.pop("vmem", 40) << 20),
        cost_estimate=pl.CostEstimate(flops=flops, bytes_accessed=nbytes, transcendentals=0),
        name=name,
        **({"out_specs": jax.tree.map(lambda _: VMEM, outs)} | grid),
    )


def mxu(a, b, dims):
    return lax.dot_general(a, b, (dims, ((), ())), preferred_element_type=jnp.float32)


def head_kernel(
    grad_hbm,
    theta_hbm,
    saved_hbm,
    degree_hbm,
    out_hbm,
    grad_ref,
    theta_ref,
    saved_ref,
    degree_ref,
    scaled_ref,
    weight_ref,
    in_sems,
    out_sems,
):
    rows, features = grad_ref.shape
    parts, _, part = scaled_ref.shape
    devices, weight_lines, _ = weight_ref.shape
    count, share = devices // parts, weight_lines // parts
    loads = [
        pltpu.make_async_copy(source, target, in_sems.at[i])
        for i, (source, target) in enumerate(
            (
                (degree_hbm, degree_ref),
                (grad_hbm, grad_ref),
                (theta_hbm, theta_ref),
                (saved_hbm, saved_ref),
            )
        )
    ]
    for load in loads:
        load.start()
    loads[0].wait()
    position = lax.axis_index("xh") * lax.axis_size("y") + lax.axis_index("y")
    start = pl.multiple_of(position * rows, rows)
    degree = degree_ref[:, pl.ds(start, rows)].astype(jnp.float32)
    down = lax.broadcasted_iota(jnp.int32, (rows, rows), 0)
    across = lax.broadcasted_iota(jnp.int32, (rows, rows), 1)
    column = jnp.sum(jnp.where(down == across, degree, 0.0), axis=1, keepdims=True)
    root = jnp.sqrt(column)
    loads[1].wait()
    loads[2].wait()
    stores = []

    def store(source, i, first, size, kind):
        stores.append(
            pltpu.make_async_copy(
                source, out_hbm.at[i, pl.ds(first, size), :], out_sems.at[kind, i]
            )
        )
        stores[-1].start()

    scaled = (mxu(grad_ref[...], theta_ref[...], ((1,), (1,))) / root).astype(scaled_ref.dtype)
    for q in range(parts):
        scaled_ref[q] = scaled[:, q * part : (q + 1) * part]
        for i in range(count):
            store(scaled_ref.at[q], q * count + i, 0, rows, 0)
    loads[3].wait()
    terms = mxu(saved_ref[...], grad_ref[...], ((0,), (0,))).astype(weight_ref.dtype)
    for i in range(devices):
        for q in range(parts):
            weight_ref[i, q * share : (q + 1) * share, :] = terms[
                i * share : (i + 1) * share, q * part : (q + 1) * part
            ]
        store(weight_ref.at[i], i, rows, weight_lines, 1)
    for copy in stores:
        copy.wait()


def own_or_other(axis, own):
    index = lax.axis_index(axis)
    return index if own else 1 - index


def sides(block):
    return own_or_other("core", block < 2), own_or_other("xh", block % 2 == 0)


def net_kernel(
    coords_ref, rows_ref, tiles_ref, keep_ref, send_ref, weight_ref, acc
):
    blocks, slots, tile_len, _ = tiles_ref.shape
    devices, lines, _ = rows_ref.shape
    depth, few, _ = weight_ref.shape
    own_rows = lines - depth * few
    per_device = own_rows // tile_len
    count = keep_ref.shape[0]
    acc[...] = jnp.zeros_like(acc)
    for block in range(blocks):
        core, high = sides(block)
        for t in range(slots):
            cell = coords_ref[0, block * slots + t]
            net = high * count + coords_ref[1, block * slots + t] * tile_len
            net = pl.multiple_of(net, tile_len)
            row = pl.multiple_of(lax.rem(cell, per_device) * tile_len, tile_len)
            source = core * (devices // 2) + lax.div(cell, per_device)
            cells = rows_ref[source, pl.ds(row, tile_len), :]
            acc[pl.ds(net, tile_len), :] += mxu(tiles_ref[block, t].T, cells, ((1,), (0,)))
    mine = pl.multiple_of(own_or_other("xl", True) * count, count)
    theirs = pl.multiple_of(own_or_other("xl", False) * count, count)
    keep_ref[...] = acc[pl.ds(mine, count), :]
    send_ref[...] = acc[pl.ds(theirs, count), :].astype(send_ref.dtype)
    weight = rows_ref[0, own_rows:, :].astype(jnp.float32)
    for i in range(1, devices):
        weight = weight + rows_ref[i, own_rows:, :].astype(jnp.float32)
    for z in range(depth):
        weight_ref[z] = weight[z * few : (z + 1) * few].astype(weight_ref.dtype)


def pack_kernel(keep_ref, came_ref, weight_ref, out_ref):
    depth = out_ref.shape[0]
    rows = keep_ref.shape[0] // depth
    for z in range(depth):
        span = slice(z * rows, (z + 1) * rows)
        summed = keep_ref[span, :] + came_ref[span, :].astype(jnp.float32)
        out_ref[z, :rows, :] = summed.astype(out_ref.dtype)
        out_ref[z, rows:, :] = weight_ref[z]


def cell_kernel(
    coords_ref, mine_ref, other_ref, tiles_ref, out_hbm, nets, acc, out_ref, sems
):
    depth, lines, _ = mine_ref.shape
    blocks, slots, tile_len, _ = tiles_ref.shape
    block_nets = nets.shape[0] // 2
    rows = block_nets // depth
    for side, ref in enumerate((mine_ref, other_ref)):
        first = own_or_other("xl", side == 0) * block_nets
        for z in range(depth):
            start = pl.multiple_of(first + z * rows, rows)
            nets[pl.ds(start, rows), :] = ref[z, :rows, :]
    devices = out_ref.shape[0]
    count = devices // 2
    per_device = acc.shape[0] // count
    few = lines - rows
    for z in range(depth):
        summed = mine_ref[z, rows:, :].astype(jnp.float32)
        summed = (summed + other_ref[z, rows:, :].astype(jnp.float32)).astype(out_ref.dtype)
        line = per_device * tile_len + z * few
        for i in range(devices):
            out_ref[i, line : line + few, :] = summed
    copies = []
    for side in range(2):
        acc[...] = jnp.zeros_like(acc)
        for block in range(side * 2, side * 2 + 2):
            core, high = sides(block)
            for t in range(slots):
                cell = coords_ref[0, block * slots + t]
                net = high * block_nets + coords_ref[1, block * slots + t] * tile_len
                net = pl.multiple_of(net, tile_len)
                acc[cell] += mxu(
                    tiles_ref[block, t], nets[pl.ds(net, tile_len), :], ((1,), (0,))
                )
        for i in range(count):
            at = side * count + i
            for j in range(per_device):
                span = slice(j * tile_len, (j + 1) * tile_len)
                out_ref[at, span, :] = acc[i * per_device + j].astype(out_ref.dtype)
            copies.append(
                pltpu.make_async_copy(out_ref.at[at], out_hbm.at[core * count + i], sems.at[at])
            )
            copies[-1].start()
    for copy in copies:
        copy.wait()


def tail_kernel(terms_ref, root_ref, cells_ref, weight_ref):
    devices, lines, part = terms_ref.shape
    rows, features = cells_ref.shape
    parts = features // part
    count, share = devices // parts, (lines - rows) // parts
    for q in range(parts):
        span = slice(q * part, (q + 1) * part)
        total = terms_ref[q * count, :rows, :].astype(jnp.float32)
        for i in range(1, count):
            total = total + terms_ref[q * count + i, :rows, :].astype(jnp.float32)
        cells_ref[:, span] = (total / root_ref[...]).astype(cells_ref.dtype)
        for i in range(devices):
            first = rows + q * share
            weight_ref[i * share : (i + 1) * share, span] = terms_ref[i, first : first + share, :]


def swap(x, axis):
    return lax.ppermute(x, axis, SWAP)


def exchange(x, axes):
    return lax.all_to_all(x, axes, 0, 0)


def tie(*values):
    return lax.optimization_barrier(values)


def shards(
    grad_out,
    saved_agg,
    theta,
    tile_values,
    tile_coords,
    block_tile_count,
    cell_degree,
    net_pin_count,
):
    own_rows, features = grad_out.shape
    block_cells = cell_degree.shape[0]
    block_nets = net_pin_count.shape[0]
    slots, tile_len = tile_values.shape[2], tile_values.shape[3]
    parts = 4
    part = features // parts
    depth = lax.axis_size("z")
    devices = lax.axis_size(PLANE)
    share_rows = block_nets // depth
    weight_lines = features // devices * parts
    few = weight_lines // depth
    lines = own_rows + weight_lines
    shape = jax.ShapeDtypeStruct
    narrow, wide = jnp.bfloat16, jnp.float32
    net_position = lax.axis_index(NETS)
    low, high = lax.axis_index("xl"), lax.axis_index("xh")

    tiles = tile_values[0]
    tiles = jnp.concatenate([tiles, swap(tiles, "xh")])
    sent = kernel_call(
        head_kernel,
        "head",
        shape((devices, lines, part), narrow),
        [
            pltpu.VMEM((own_rows, features), narrow),
            pltpu.VMEM((features, features), narrow),
            pltpu.VMEM((own_rows, features), narrow),
            pltpu.VMEM((1, block_cells), jnp.int32),
            pltpu.VMEM((parts, own_rows, part), narrow),
            pltpu.VMEM((devices, weight_lines, part), narrow),
            pltpu.SemaphoreType.DMA((4,)),
            pltpu.SemaphoreType.DMA((2, devices)),
        ],
        4 * own_rows * features * features,
        4 << 20,
        [HBM, HBM, HBM, HBM],
        out_specs=HBM,
        vmem=60,
    )(grad_out, theta, saved_agg, cell_degree.reshape(1, block_cells))
    tile_coords, block_tile_count, net_pin_count, sent = tie(
        tile_coords, block_tile_count, net_pin_count, sent
    )
    gathered = exchange(sent, PLANE)

    own = jnp.concatenate(
        [tile_coords[0, 0].T, jnp.broadcast_to(block_tile_count, (1, slots))]
    )
    across = lax.ppermute(own, ("core", "xh"), [(i, 3 - i) for i in range(4)])
    coords = jnp.concatenate([own, swap(own, "xh"), swap(own, "core"), across], axis=1)
    tiles = jnp.concatenate([tiles, swap(tiles, "core")])
    live = jnp.arange(slots, dtype=jnp.int32) < coords[2].reshape(4, slots)
    tiles = jnp.where(live[:, :, None, None], tiles, jnp.zeros((), narrow))
    pins = jnp.where(low == high, net_pin_count, swap(net_pin_count, "xh"))
    pins = pins.astype(wide).reshape(depth, share_rows)
    pins = lax.dynamic_index_in_dim(pins, lax.axis_index("z"), 0, False)[:, None]
    divisor = jnp.concatenate([pins, jnp.ones((few, 1), wide)], axis=0)
    own_degree = lax.dynamic_slice_in_dim(cell_degree, net_position * own_rows, own_rows)
    own_root = jnp.sqrt(own_degree.astype(wide))[:, None]
    gathered, tiles, coords, divisor, own_root = tie(gathered, tiles, coords, divisor, own_root)

    keep, sent, weight = kernel_call(
        net_kernel,
        "net_sums",
        (
            shape((block_nets, part), wide),
            shape((block_nets, part), narrow),
            shape((depth, few, part), narrow),
        ),
        [pltpu.VMEM((2 * block_nets, part), wide)],
        8 * slots * tile_len * tile_len * part,
        5 << 20,
        [SMEM, VMEM, VMEM],
    )(coords, gathered, tiles)
    terms = kernel_call(
        pack_kernel,
        "pack",
        shape((depth, share_rows + few, part), narrow),
        [],
        0,
        1 << 20,
        [VMEM, VMEM, VMEM],
    )(keep, swap(sent, "xl"), weight)
    summed = jnp.sum(exchange(terms, "z").astype(wide), axis=0)
    share = (summed / divisor).astype(narrow)
    mine = exchange(jnp.broadcast_to(share[None], terms.shape), "z")
    other = swap(mine, "xl")
    cell_terms = kernel_call(
        cell_kernel,
        "cell_terms",
        shape((devices, lines, part), narrow),
        [
            pltpu.VMEM((2 * block_nets, part), narrow),
            pltpu.VMEM((block_cells // tile_len, tile_len, part), wide),
            pltpu.VMEM((devices, lines, part), narrow),
            pltpu.SemaphoreType.DMA((devices,)),
        ],
        8 * slots * tile_len * tile_len * part,
        4 << 20,
        [SMEM, VMEM, VMEM, VMEM],
        out_specs=HBM,
        vmem=60,
    )(coords, mine, other, tiles)
    return kernel_call(
        tail_kernel,
        "tail",
        (shape(grad_out.shape, narrow), shape((features, features), narrow)),
        [],
        0,
        4 << 20,
        [VMEM, VMEM],
    )(exchange(cell_terms, PLANE), own_root)


def solution(mesh):
    cells, nets = mesh.devices.shape
    fine = Mesh(mesh.devices.reshape(cells // 4, 2, 2, 2, nets // 2), CELLS + NETS)
    every = CELLS + NETS
    in_specs = (
        P(every, None),
        P(every, None),
        P(),
        P(CELLS, NETS, None, None, None),
        P(CELLS, NETS, None, None),
        P(CELLS, NETS),
        P(CELLS),
        P(NETS),
    )
    out_specs = (P(every, None), P())
    return jax.shard_map(shards, mesh=fine, in_specs=in_specs, out_specs=out_specs, check_vma=False)
```

```python
import functools

import jax
import jax.numpy as jnp
from jax import lax
from jax.experimental import pallas as pl
from jax.experimental.pallas import tpu as pltpu
from jax.sharding import Mesh
from jax.sharding import PartitionSpec as P

SWAP = ((0, 1), (1, 0))
CELLS = ("z", "xl", "core")
NETS = ("xh", "y")
PLANE = ("core",) + NETS
SMEM = pl.BlockSpec(memory_space=pltpu.SMEM)
VMEM = pl.BlockSpec(memory_space=pltpu.VMEM)
HBM = pl.BlockSpec(memory_space=pltpu.HBM)


def kernel_call(body, name, outs, scratch, flops, nbytes, ins, **grid):
    return pl.pallas_call(
        body,
        out_shape=outs,
        in_specs=ins,
        scratch_shapes=scratch,
        compiler_params=pltpu.CompilerParams(vmem_limit_bytes=grid.pop("vmem", 40) << 20),
        cost_estimate=pl.CostEstimate(flops=flops, bytes_accessed=nbytes, transcendentals=0),
        name=name,
        **({"out_specs": jax.tree.map(lambda _: VMEM, outs)} | grid),
    )


def mxu(a, b, dims):
    return lax.dot_general(a, b, (dims, ((), ())), preferred_element_type=jnp.float32)


def head_kernel(
    grad_hbm,
    theta_hbm,
    saved_hbm,
    degree_hbm,
    out_hbm,
    grad_ref,
    theta_ref,
    saved_ref,
    degree_ref,
    scaled_ref,
    weight_ref,
    in_sems,
    out_sems,
):
    rows, features = grad_ref.shape
    parts, _, part = scaled_ref.shape
    devices, weight_lines, _ = weight_ref.shape
    count, share = devices // parts, weight_lines // parts
    loads = [
        pltpu.make_async_copy(source, target, in_sems.at[i])
        for i, (source, target) in enumerate(
            (
                (degree_hbm, degree_ref),
                (grad_hbm, grad_ref),
                (theta_hbm, theta_ref),
                (saved_hbm, saved_ref),
            )
        )
    ]
    for load in loads:
        load.start()
    loads[0].wait()
    position = lax.axis_index("xh") * lax.axis_size("y") + lax.axis_index("y")
    start = pl.multiple_of(position * rows, rows)
    degree = degree_ref[:, pl.ds(start, rows)].astype(jnp.float32)
    down = lax.broadcasted_iota(jnp.int32, (rows, rows), 0)
    across = lax.broadcasted_iota(jnp.int32, (rows, rows), 1)
    column = jnp.sum(jnp.where(down == across, degree, 0.0), axis=1, keepdims=True)
    root = jnp.sqrt(column)
    loads[1].wait()
    loads[2].wait()
    stores = []

    def store(source, i, first, size, kind):
        stores.append(
            pltpu.make_async_copy(
                source, out_hbm.at[i, pl.ds(first, size), :], out_sems.at[kind, i]
            )
        )
        stores[-1].start()

    scaled = (mxu(grad_ref[...], theta_ref[...], ((1,), (1,))) / root).astype(scaled_ref.dtype)
    for q in range(parts):
        scaled_ref[q] = scaled[:, q * part : (q + 1) * part]
        for i in range(count):
            store(scaled_ref.at[q], q * count + i, 0, rows, 0)
    loads[3].wait()
    terms = mxu(saved_ref[...], grad_ref[...], ((0,), (0,))).astype(weight_ref.dtype)
    for i in range(devices):
        for q in range(parts):
            weight_ref[i, q * share : (q + 1) * share, :] = terms[
                i * share : (i + 1) * share, q * part : (q + 1) * part
            ]
        store(weight_ref.at[i], i, rows, weight_lines, 1)
    for copy in stores:
        copy.wait()


def own_or_other(axis, own):
    index = lax.axis_index(axis)
    return index if own else 1 - index


def add_net_sums(coords_ref, rows_ref, tiles_ref, others_ref, acc, own, own_rows):
    slots, tile_len = tiles_ref.shape[1:3]
    devices = rows_ref.shape[0]
    per_device = own_rows // tile_len
    spare = acc.shape[0] - tile_len
    acc[...] = jnp.zeros_like(acc)
    pick = lax.rem(own_or_other("xl", own) + lax.axis_index("xh"), 2)
    for side, ref in enumerate((tiles_ref, others_ref)):
        core = own_or_other("core", side == 0)
        first = (2 * side + pick) * slots
        count = coords_ref[2, first]
        for t in range(slots):
            cell = coords_ref[0, first + t]
            net = jnp.where(t < count, coords_ref[1, first + t] * tile_len, spare)
            net = pl.multiple_of(net, tile_len)
            row = pl.multiple_of(lax.rem(cell, per_device) * tile_len, tile_len)
            source = core * (devices // 2) + lax.div(cell, per_device)
            cells = rows_ref[source, pl.ds(row, tile_len), :]
            acc[pl.ds(net, tile_len), :] += mxu(ref[pick, t].T, cells, ((1,), (0,)))


def own_or_other(axis, own):
    index = lax.axis_index(axis)
    return index if own else 1 - index


def send_kernel(own_rows, coords_ref, rows_ref, tiles_ref, others_ref, send_ref, acc):
    add_net_sums(coords_ref, rows_ref, tiles_ref, others_ref, acc, False, own_rows)
    send_ref[...] = acc[: send_ref.shape[0], :].astype(send_ref.dtype)


def keep_kernel(own_rows, coords_ref, rows_ref, tiles_ref, others_ref, keep_ref, weight_ref, acc):
    add_net_sums(coords_ref, rows_ref, tiles_ref, others_ref, acc, True, own_rows)
    keep_ref[...] = acc[: keep_ref.shape[0], :]
    depth, few, _ = weight_ref.shape
    weight = rows_ref[0, own_rows:, :].astype(jnp.float32)
    for i in range(1, rows_ref.shape[0]):
        weight = weight + rows_ref[i, own_rows:, :].astype(jnp.float32)
    for z in range(depth):
        weight_ref[z] = weight[z * few : (z + 1) * few].astype(weight_ref.dtype)


def pack_kernel(keep_ref, came_ref, weight_ref, out_ref):
    depth = out_ref.shape[0]
    rows = keep_ref.shape[0] // depth
    for z in range(depth):
        span = slice(z * rows, (z + 1) * rows)
        summed = keep_ref[span, :] + came_ref[span, :].astype(jnp.float32)
        out_ref[z, :rows, :] = summed.astype(out_ref.dtype)
        out_ref[z, rows:, :] = weight_ref[z]


def cell_kernel(
    coords_ref, mine_ref, other_ref, tiles_ref, others_ref, out_hbm, nets, acc, out_ref, sems
):
    depth, lines, _ = mine_ref.shape
    slots, tile_len = tiles_ref.shape[1:3]
    block_nets = nets.shape[0] // 2
    rows = block_nets // depth
    for side, ref in enumerate((mine_ref, other_ref)):
        first = own_or_other("xl", side == 0) * block_nets
        for z in range(depth):
            start = pl.multiple_of(first + z * rows, rows)
            nets[pl.ds(start, rows), :] = ref[z, :rows, :]
    devices = out_ref.shape[0]
    count = devices // 2
    spare = acc.shape[0] - 1
    per_device = spare // count
    few = lines - rows
    for z in range(depth):
        summed = mine_ref[z, rows:, :].astype(jnp.float32)
        summed = (summed + other_ref[z, rows:, :].astype(jnp.float32)).astype(out_ref.dtype)
        line = per_device * tile_len + z * few
        for i in range(devices):
            out_ref[i, line : line + few, :] = summed
    copies = []
    for side, ref in enumerate((tiles_ref, others_ref)):
        core = own_or_other("core", side == 0)
        acc[...] = jnp.zeros_like(acc)
        for pair in range(2):
            high = own_or_other("xh", pair == 0)
            first = (2 * side + pair) * slots
            live = coords_ref[2, first]
            for t in range(slots):
                cell = jnp.where(t < live, coords_ref[0, first + t], spare)
                net = high * block_nets + coords_ref[1, first + t] * tile_len
                net = pl.multiple_of(net, tile_len)
                acc[cell] += mxu(ref[pair, t], nets[pl.ds(net, tile_len), :], ((1,), (0,)))
        for i in range(count):
            at = side * count + i
            for j in range(per_device):
                span = slice(j * tile_len, (j + 1) * tile_len)
                out_ref[at, span, :] = acc[i * per_device + j].astype(out_ref.dtype)
            copies.append(
                pltpu.make_async_copy(out_ref.at[at], out_hbm.at[core * count + i], sems.at[at])
            )
            copies[-1].start()
    for copy in copies:
        copy.wait()


def tail_kernel(terms_ref, root_ref, cells_ref, weight_ref):
    devices, lines, part = terms_ref.shape
    rows, features = cells_ref.shape
    parts = features // part
    count, share = devices // parts, (lines - rows) // parts
    for q in range(parts):
        span = slice(q * part, (q + 1) * part)
        total = terms_ref[q * count, :rows, :].astype(jnp.float32)
        for i in range(1, count):
            total = total + terms_ref[q * count + i, :rows, :].astype(jnp.float32)
        cells_ref[:, span] = (total / root_ref[...]).astype(cells_ref.dtype)
        for i in range(devices):
            first = rows + q * share
            weight_ref[i * share : (i + 1) * share, span] = terms_ref[i, first : first + share, :]


def swap(x, axis):
    return lax.ppermute(x, axis, SWAP)


def exchange(x, axes):
    return lax.all_to_all(x, axes, 0, 0)


def tie(*values):
    return lax.optimization_barrier(values)


def shards(
    grad_out,
    saved_agg,
    theta,
    tile_values,
    tile_coords,
    block_tile_count,
    cell_degree,
    net_pin_count,
):
    own_rows, features = grad_out.shape
    block_cells = cell_degree.shape[0]
    block_nets = net_pin_count.shape[0]
    slots, tile_len = tile_values.shape[2], tile_values.shape[3]
    parts = 4
    part = features // parts
    depth = lax.axis_size("z")
    devices = lax.axis_size(PLANE)
    share_rows = block_nets // depth
    weight_lines = features // devices * parts
    few = weight_lines // depth
    lines = own_rows + weight_lines
    shape = jax.ShapeDtypeStruct
    narrow, wide = jnp.bfloat16, jnp.float32
    net_position = lax.axis_index(NETS)
    low, high = lax.axis_index("xl"), lax.axis_index("xh")

    tiles = tile_values[0]
    tiles = jnp.concatenate([tiles, swap(tiles, "xh")])
    sent = kernel_call(
        head_kernel,
        "head",
        shape((devices, lines, part), narrow),
        [
            pltpu.VMEM((own_rows, features), narrow),
            pltpu.VMEM((features, features), narrow),
            pltpu.VMEM((own_rows, features), narrow),
            pltpu.VMEM((1, block_cells), jnp.int32),
            pltpu.VMEM((parts, own_rows, part), narrow),
            pltpu.VMEM((devices, weight_lines, part), narrow),
            pltpu.SemaphoreType.DMA((4,)),
            pltpu.SemaphoreType.DMA((2, devices)),
        ],
        4 * own_rows * features * features,
        4 << 20,
        [HBM, HBM, HBM, HBM],
        out_specs=HBM,
        vmem=60,
    )(grad_out, theta, saved_agg, cell_degree.reshape(1, block_cells))
    tile_coords, block_tile_count, sent = tie(tile_coords, block_tile_count, sent)
    gathered = exchange(sent, PLANE)

    own = jnp.concatenate(
        [tile_coords[0, 0].T, jnp.broadcast_to(block_tile_count, (1, slots))]
    )
    across = lax.ppermute(own, ("core", "xh"), [(i, 3 - i) for i in range(4)])
    coords = jnp.concatenate([own, swap(own, "xh"), swap(own, "core"), across], axis=1)
    others = swap(tiles, "core")
    own_degree = lax.dynamic_slice_in_dim(cell_degree, net_position * own_rows, own_rows)
    own_root = jnp.sqrt(own_degree.astype(wide))[:, None]
    gathered, tiles, others, coords, own_root = tie(gathered, tiles, others, coords, own_root)

    def net_sums(body, name, outs):
        return kernel_call(
            functools.partial(body, own_rows),
            name,
            outs,
            [pltpu.VMEM((block_nets + tile_len, part), wide)],
            4 * slots * tile_len * tile_len * part,
            3 << 20,
            [SMEM, VMEM, VMEM, VMEM],
        )(coords, gathered, tiles, others)

    sent = net_sums(send_kernel, "sent_sums", shape((block_nets, part), narrow))
    came = swap(sent, "xl")
    net_pin_count, sent = tie(net_pin_count, sent)
    keep, weight = net_sums(
        keep_kernel,
        "kept_sums",
        (shape((block_nets, part), wide), shape((depth, few, part), narrow)),
    )
    pins = jnp.where(low == high, net_pin_count, swap(net_pin_count, "xh"))
    pins = pins.astype(wide).reshape(depth, share_rows)
    pins = lax.dynamic_index_in_dim(pins, lax.axis_index("z"), 0, False)[:, None]
    divisor = jnp.concatenate([pins, jnp.ones((few, 1), wide)], axis=0)
    came, divisor, keep = tie(came, divisor, keep)
    terms = kernel_call(
        pack_kernel,
        "pack",
        shape((depth, share_rows + few, part), narrow),
        [],
        0,
        1 << 20,
        [VMEM, VMEM, VMEM],
    )(keep, came, weight)
    summed = jnp.sum(exchange(terms, "z").astype(wide), axis=0)
    share = (summed / divisor).astype(narrow)
    mine = exchange(jnp.broadcast_to(share[None], terms.shape), "z")
    other = swap(mine, "xl")
    cell_terms = kernel_call(
        cell_kernel,
        "cell_terms",
        shape((devices, lines, part), narrow),
        [
            pltpu.VMEM((2 * block_nets, part), narrow),
            pltpu.VMEM((block_cells // tile_len + 1, tile_len, part), wide),
            pltpu.VMEM((devices, lines, part), narrow),
            pltpu.SemaphoreType.DMA((devices,)),
        ],
        8 * slots * tile_len * tile_len * part,
        4 << 20,
        [SMEM, VMEM, VMEM, VMEM, VMEM],
        out_specs=HBM,
        vmem=60,
    )(coords, mine, other, tiles, others)
    return kernel_call(
        tail_kernel,
        "tail",
        (shape(grad_out.shape, narrow), shape((features, features), narrow)),
        [],
        0,
        4 << 20,
        [VMEM, VMEM],
    )(exchange(cell_terms, PLANE), own_root)


def solution(mesh):
    cells, nets = mesh.devices.shape
    fine = Mesh(mesh.devices.reshape(cells // 4, 2, 2, 2, nets // 2), CELLS + NETS)
    every = CELLS + NETS
    in_specs = (
        P(every, None),
        P(every, None),
        P(),
        P(CELLS, NETS, None, None, None),
        P(CELLS, NETS, None, None),
        P(CELLS, NETS),
        P(CELLS),
        P(NETS),
    )
    out_specs = (P(every, None), P())
    return jax.shard_map(shards, mesh=fine, in_specs=in_specs, out_specs=out_specs, check_vma=False)
```

```python
import functools

import jax
import jax.numpy as jnp
from jax import lax
from jax.experimental import pallas as pl
from jax.experimental.pallas import tpu as pltpu
from jax.sharding import Mesh
from jax.sharding import PartitionSpec as P

SWAP = ((0, 1), (1, 0))
CELLS = ("z", "xl", "core")
NETS = ("xh", "y")
PLANE = ("core",) + NETS
SMEM = pl.BlockSpec(memory_space=pltpu.SMEM)
VMEM = pl.BlockSpec(memory_space=pltpu.VMEM)
HBM = pl.BlockSpec(memory_space=pltpu.HBM)


def kernel_call(body, name, outs, scratch, flops, nbytes, ins, **grid):
    return pl.pallas_call(
        body,
        out_shape=outs,
        in_specs=ins,
        scratch_shapes=scratch,
        compiler_params=pltpu.CompilerParams(vmem_limit_bytes=grid.pop("vmem", 40) << 20),
        cost_estimate=pl.CostEstimate(flops=flops, bytes_accessed=nbytes, transcendentals=0),
        name=name,
        **({"out_specs": jax.tree.map(lambda _: VMEM, outs)} | grid),
    )


def mxu(a, b, dims):
    return lax.dot_general(a, b, (dims, ((), ())), preferred_element_type=jnp.float32)


def head_kernel(
    grad_hbm,
    theta_hbm,
    saved_hbm,
    degree_hbm,
    out_hbm,
    grad_ref,
    theta_ref,
    saved_ref,
    degree_ref,
    scaled_ref,
    weight_ref,
    in_sems,
    out_sems,
):
    rows, features = grad_ref.shape
    parts, _, part = scaled_ref.shape
    devices, weight_lines, _ = weight_ref.shape
    count, share = devices // parts, weight_lines // parts
    loads = [
        pltpu.make_async_copy(source, target, in_sems.at[i])
        for i, (source, target) in enumerate(
            (
                (degree_hbm, degree_ref),
                (grad_hbm, grad_ref),
                (theta_hbm, theta_ref),
                (saved_hbm, saved_ref),
            )
        )
    ]
    for load in loads:
        load.start()
    loads[0].wait()
    position = lax.axis_index("xh") * lax.axis_size("y") + lax.axis_index("y")
    start = pl.multiple_of(position * rows, rows)
    degree = degree_ref[:, pl.ds(start, rows)].astype(jnp.float32)
    down = lax.broadcasted_iota(jnp.int32, (rows, rows), 0)
    across = lax.broadcasted_iota(jnp.int32, (rows, rows), 1)
    column = jnp.sum(jnp.where(down == across, degree, 0.0), axis=1, keepdims=True)
    root = jnp.sqrt(column)
    loads[1].wait()
    loads[2].wait()
    stores = []

    def store(source, i, first, size, kind):
        stores.append(
            pltpu.make_async_copy(
                source, out_hbm.at[i, pl.ds(first, size), :], out_sems.at[kind, i]
            )
        )
        stores[-1].start()

    scaled = (mxu(grad_ref[...], theta_ref[...], ((1,), (1,))) / root).astype(scaled_ref.dtype)
    for q in range(parts):
        scaled_ref[q] = scaled[:, q * part : (q + 1) * part]
        for i in range(count):
            store(scaled_ref.at[q], q * count + i, 0, rows, 0)
    loads[3].wait()
    terms = mxu(saved_ref[...], grad_ref[...], ((0,), (0,))).astype(weight_ref.dtype)
    for i in range(devices):
        for q in range(parts):
            weight_ref[i, q * share : (q + 1) * share, :] = terms[
                i * share : (i + 1) * share, q * part : (q + 1) * part
            ]
        store(weight_ref.at[i], i, rows, weight_lines, 1)
    for copy in stores:
        copy.wait()


def own_or_other(axis, own):
    index = lax.axis_index(axis)
    return index if own else 1 - index


def add_net_sums(coords_ref, rows_ref, tiles_ref, others_ref, acc, own, own_rows):
    slots, tile_len = tiles_ref.shape[1:3]
    devices = rows_ref.shape[0]
    per_device = own_rows // tile_len
    spare = acc.shape[0] - tile_len
    acc[...] = jnp.zeros_like(acc)
    pick = lax.rem(own_or_other("xl", own) + lax.axis_index("xh"), 2)
    for side, ref in enumerate((tiles_ref, others_ref)):
        core = own_or_other("core", side == 0)
        first = (2 * side + pick) * slots
        count = coords_ref[2, first]
        for t in range(slots):
            cell = coords_ref[0, first + t]
            net = jnp.where(t < count, coords_ref[1, first + t] * tile_len, spare)
            net = pl.multiple_of(net, tile_len)
            row = pl.multiple_of(lax.rem(cell, per_device) * tile_len, tile_len)
            source = core * (devices // 2) + lax.div(cell, per_device)
            cells = rows_ref[source, pl.ds(row, tile_len), :]
            acc[pl.ds(net, tile_len), :] += mxu(ref[pick, t].T, cells, ((1,), (0,)))


def own_or_other(axis, own):
    index = lax.axis_index(axis)
    return index if own else 1 - index


def send_kernel(own_rows, coords_ref, rows_ref, tiles_ref, others_ref, send_ref, acc):
    add_net_sums(coords_ref, rows_ref, tiles_ref, others_ref, acc, False, own_rows)
    send_ref[...] = acc[: send_ref.shape[0], :].astype(send_ref.dtype)


def keep_kernel(own_rows, coords_ref, rows_ref, tiles_ref, others_ref, keep_ref, weight_ref, acc):
    add_net_sums(coords_ref, rows_ref, tiles_ref, others_ref, acc, True, own_rows)
    keep_ref[...] = acc[: keep_ref.shape[0], :]
    depth, few, _ = weight_ref.shape
    weight = rows_ref[0, own_rows:, :].astype(jnp.float32)
    for i in range(1, rows_ref.shape[0]):
        weight = weight + rows_ref[i, own_rows:, :].astype(jnp.float32)
    for z in range(depth):
        weight_ref[z] = weight[z * few : (z + 1) * few].astype(weight_ref.dtype)


def pack_kernel(keep_ref, came_ref, weight_ref, out_ref):
    depth = out_ref.shape[0]
    rows = keep_ref.shape[0] // depth
    for z in range(depth):
        span = slice(z * rows, (z + 1) * rows)
        summed = keep_ref[span, :] + came_ref[span, :].astype(jnp.float32)
        out_ref[z, :rows, :] = summed.astype(out_ref.dtype)
        out_ref[z, rows:, :] = weight_ref[z]


def cell_kernel(
    coords_ref, mine_ref, other_ref, tiles_ref, others_ref, out_hbm, nets, acc, out_ref, sems
):
    depth, lines, _ = mine_ref.shape
    slots, tile_len = tiles_ref.shape[1:3]
    block_nets = nets.shape[0] // 2
    rows = block_nets // depth
    for side, ref in enumerate((mine_ref, other_ref)):
        first = own_or_other("xl", side == 0) * block_nets
        for z in range(depth):
            start = pl.multiple_of(first + z * rows, rows)
            nets[pl.ds(start, rows), :] = ref[z, :rows, :]
    devices = out_ref.shape[0]
    count = devices // 2
    spare = acc.shape[0] - 1
    per_device = spare // count
    few = lines - rows
    for z in range(depth):
        summed = mine_ref[z, rows:, :].astype(jnp.float32)
        summed = (summed + other_ref[z, rows:, :].astype(jnp.float32)).astype(out_ref.dtype)
        line = per_device * tile_len + z * few
        for i in range(devices):
            out_ref[i, line : line + few, :] = summed
    copies = []
    for side, ref in enumerate((tiles_ref, others_ref)):
        core = own_or_other("core", side == 0)
        acc[...] = jnp.zeros_like(acc)
        for pair in range(2):
            high = own_or_other("xh", pair == 0)
            first = (2 * side + pair) * slots
            live = coords_ref[2, first]
            for t in range(slots):
                cell = jnp.where(t < live, coords_ref[0, first + t], spare)
                net = high * block_nets + coords_ref[1, first + t] * tile_len
                net = pl.multiple_of(net, tile_len)
                acc[cell] += mxu(ref[pair, t], nets[pl.ds(net, tile_len), :], ((1,), (0,)))
        for i in range(count):
            at = side * count + i
            for j in range(per_device):
                span = slice(j * tile_len, (j + 1) * tile_len)
                out_ref[at, span, :] = acc[i * per_device + j].astype(out_ref.dtype)
            copies.append(
                pltpu.make_async_copy(out_ref.at[at], out_hbm.at[core * count + i], sems.at[at])
            )
            copies[-1].start()
    for copy in copies:
        copy.wait()


def tail_kernel(terms_ref, root_ref, cells_ref, weight_ref):
    devices, lines, part = terms_ref.shape
    rows, features = cells_ref.shape
    parts = features // part
    count, share = devices // parts, (lines - rows) // parts
    for q in range(parts):
        span = slice(q * part, (q + 1) * part)
        total = terms_ref[q * count, :rows, :].astype(jnp.float32)
        for i in range(1, count):
            total = total + terms_ref[q * count + i, :rows, :].astype(jnp.float32)
        cells_ref[:, span] = (total / root_ref[...]).astype(cells_ref.dtype)
        for i in range(devices):
            first = rows + q * share
            weight_ref[i * share : (i + 1) * share, span] = terms_ref[i, first : first + share, :]


def swap(x, axis):
    return lax.ppermute(x, axis, SWAP)


def exchange(x, axes):
    return lax.all_to_all(x, axes, 0, 0)


def tie(*values):
    return lax.optimization_barrier(values)


def shards(
    grad_out,
    saved_agg,
    theta,
    tile_values,
    tile_coords,
    block_tile_count,
    cell_degree,
    net_pin_count,
):
    own_rows, features = grad_out.shape
    block_cells = cell_degree.shape[0]
    block_nets = net_pin_count.shape[0]
    slots, tile_len = tile_values.shape[2], tile_values.shape[3]
    parts = 4
    part = features // parts
    depth = lax.axis_size("z")
    devices = lax.axis_size(PLANE)
    share_rows = block_nets // depth
    weight_lines = features // devices * parts
    few = weight_lines // depth
    lines = own_rows + weight_lines
    shape = jax.ShapeDtypeStruct
    narrow, wide = jnp.bfloat16, jnp.float32
    net_position = lax.axis_index(NETS)
    low, high = lax.axis_index("xl"), lax.axis_index("xh")

    tiles = tile_values[0]
    tiles = jnp.concatenate([tiles, swap(tiles, "xh")])
    sent = kernel_call(
        head_kernel,
        "head",
        shape((devices, lines, part), narrow),
        [
            pltpu.VMEM((own_rows, features), narrow),
            pltpu.VMEM((features, features), narrow),
            pltpu.VMEM((own_rows, features), narrow),
            pltpu.VMEM((1, block_cells), jnp.int32),
            pltpu.VMEM((parts, own_rows, part), narrow),
            pltpu.VMEM((devices, weight_lines, part), narrow),
            pltpu.SemaphoreType.DMA((4,)),
            pltpu.SemaphoreType.DMA((2, devices)),
        ],
        4 * own_rows * features * features,
        4 << 20,
        [HBM, HBM, HBM, HBM],
        out_specs=HBM,
        vmem=60,
    )(grad_out, theta, saved_agg, cell_degree.reshape(1, block_cells))
    tile_coords, block_tile_count, sent = tie(tile_coords, block_tile_count, sent)
    gathered = exchange(sent, PLANE)

    own = jnp.concatenate(
        [tile_coords[0, 0].T, jnp.broadcast_to(block_tile_count, (1, slots))]
    )
    across = lax.ppermute(own, ("core", "xh"), [(i, 3 - i) for i in range(4)])
    coords = jnp.concatenate([own, swap(own, "xh"), swap(own, "core"), across], axis=1)
    others = swap(tiles, "core")
    own_degree = lax.dynamic_slice_in_dim(cell_degree, net_position * own_rows, own_rows)
    own_root = jnp.sqrt(own_degree.astype(wide))[:, None]
    gathered, tiles, others, coords, own_root = tie(gathered, tiles, others, coords, own_root)

    def net_sums(body, name, outs):
        return kernel_call(
            functools.partial(body, own_rows),
            name,
            outs,
            [pltpu.VMEM((block_nets + tile_len, part), wide)],
            4 * slots * tile_len * tile_len * part,
            3 << 20,
            [SMEM, VMEM, VMEM, VMEM],
        )(coords, gathered, tiles, others)

    sent = net_sums(send_kernel, "sent_sums", shape((block_nets, part), narrow))
    came = swap(sent, "xl")
    net_pin_count, sent = tie(net_pin_count, sent)
    keep, weight = net_sums(
        keep_kernel,
        "kept_sums",
        (shape((block_nets, part), wide), shape((depth, few, part), narrow)),
    )
    pins = jnp.where(low == high, net_pin_count, swap(net_pin_count, "xh"))
    pins = pins.astype(wide).reshape(depth, share_rows)
    pins = lax.dynamic_index_in_dim(pins, lax.axis_index("z"), 0, False)[:, None]
    divisor = jnp.concatenate([pins, jnp.ones((few, 1), wide)], axis=0)
    came, divisor, keep = tie(came, divisor, keep)
    terms = kernel_call(
        pack_kernel,
        "pack",
        shape((depth, share_rows + few, part), narrow),
        [],
        0,
        1 << 20,
        [VMEM, VMEM, VMEM],
    )(keep, came, weight)
    summed = jnp.sum(exchange(terms, "z").astype(wide), axis=0)
    share = (summed / divisor).astype(narrow)
    mine = exchange(jnp.broadcast_to(share[None], terms.shape), "z")
    other = swap(mine, "xl")
    cell_terms = kernel_call(
        cell_kernel,
        "cell_terms",
        shape((devices, lines, part), narrow),
        [
            pltpu.VMEM((2 * block_nets, part), narrow),
            pltpu.VMEM((block_cells // tile_len + 1, tile_len, part), wide),
            pltpu.VMEM((devices, lines, part), narrow),
            pltpu.SemaphoreType.DMA((devices,)),
        ],
        8 * slots * tile_len * tile_len * part,
        4 << 20,
        [SMEM, VMEM, VMEM, VMEM, VMEM],
        out_specs=HBM,
        vmem=40,
    )(coords, mine, other, tiles, others)
    return kernel_call(
        tail_kernel,
        "tail",
        (shape(grad_out.shape, narrow), shape((features, features), narrow)),
        [],
        0,
        4 << 20,
        [VMEM, VMEM],
    )(exchange(cell_terms, PLANE), own_root)


def solution(mesh):
    cells, nets = mesh.devices.shape
    fine = Mesh(mesh.devices.reshape(cells // 4, 2, 2, 2, nets // 2), CELLS + NETS)
    every = CELLS + NETS
    in_specs = (
        P(every, None),
        P(every, None),
        P(),
        P(CELLS, NETS, None, None, None),
        P(CELLS, NETS, None, None),
        P(CELLS, NETS),
        P(CELLS),
        P(NETS),
    )
    out_specs = (P(every, None), P())
    return jax.shard_map(shards, mesh=fine, in_specs=in_specs, out_specs=out_specs, check_vma=False)
```

```python
import functools

import jax
import jax.numpy as jnp
from jax import lax
from jax.experimental import pallas as pl
from jax.experimental.pallas import tpu as pltpu
from jax.sharding import Mesh
from jax.sharding import PartitionSpec as P

SWAP = ((0, 1), (1, 0))
CELLS = ("z", "xl", "core")
NETS = ("xh", "y")
PLANE = ("core",) + NETS
SMEM = pl.BlockSpec(memory_space=pltpu.SMEM)
VMEM = pl.BlockSpec(memory_space=pltpu.VMEM)
HBM = pl.BlockSpec(memory_space=pltpu.HBM)


def kernel_call(body, name, outs, scratch, flops, nbytes, ins, **grid):
    return pl.pallas_call(
        body,
        out_shape=outs,
        in_specs=ins,
        scratch_shapes=scratch,
        compiler_params=pltpu.CompilerParams(vmem_limit_bytes=grid.pop("vmem", 40) << 20),
        cost_estimate=pl.CostEstimate(flops=flops, bytes_accessed=nbytes, transcendentals=0),
        name=name,
        **({"out_specs": jax.tree.map(lambda _: VMEM, outs)} | grid),
    )


def mxu(a, b, dims):
    return lax.dot_general(a, b, (dims, ((), ())), preferred_element_type=jnp.float32)


def head_kernel(
    grad_hbm,
    theta_hbm,
    saved_hbm,
    degree_hbm,
    out_hbm,
    grad_ref,
    theta_ref,
    saved_ref,
    degree_ref,
    scaled_ref,
    weight_ref,
    in_sems,
    out_sems,
):
    rows, features = grad_ref.shape
    parts, _, part = scaled_ref.shape
    devices, weight_lines, _ = weight_ref.shape
    count, share = devices // parts, weight_lines // parts
    loads = [
        pltpu.make_async_copy(source, target, in_sems.at[i])
        for i, (source, target) in enumerate(
            (
                (degree_hbm, degree_ref),
                (grad_hbm, grad_ref),
                (theta_hbm, theta_ref),
                (saved_hbm, saved_ref),
            )
        )
    ]
    for load in loads:
        load.start()
    loads[0].wait()
    position = lax.axis_index("xh") * lax.axis_size("y") + lax.axis_index("y")
    start = pl.multiple_of(position * rows, rows)
    degree = degree_ref[:, pl.ds(start, rows)].astype(jnp.float32)
    down = lax.broadcasted_iota(jnp.int32, (rows, rows), 0)
    across = lax.broadcasted_iota(jnp.int32, (rows, rows), 1)
    column = jnp.sum(jnp.where(down == across, degree, 0.0), axis=1, keepdims=True)
    root = jnp.sqrt(column)
    loads[1].wait()
    loads[2].wait()
    stores = []

    def store(source, i, first, size, kind):
        stores.append(
            pltpu.make_async_copy(
                source, out_hbm.at[i, pl.ds(first, size), :], out_sems.at[kind, i]
            )
        )
        stores[-1].start()

    scaled = (mxu(grad_ref[...], theta_ref[...], ((1,), (1,))) / root).astype(scaled_ref.dtype)
    for q in range(parts):
        scaled_ref[q] = scaled[:, q * part : (q + 1) * part]
        for i in range(count):
            store(scaled_ref.at[q], q * count + i, 0, rows, 0)
    loads[3].wait()
    terms = mxu(saved_ref[...], grad_ref[...], ((0,), (0,))).astype(weight_ref.dtype)
    for i in range(devices):
        for q in range(parts):
            weight_ref[i, q * share : (q + 1) * share, :] = terms[
                i * share : (i + 1) * share, q * part : (q + 1) * part
            ]
        store(weight_ref.at[i], i, rows, weight_lines, 1)
    for copy in stores:
        copy.wait()


def own_or_other(axis, own):
    index = lax.axis_index(axis)
    return index if own else 1 - index


def add_net_sums(coords_ref, rows_ref, tiles_ref, others_ref, acc, own, own_rows):
    slots, tile_len = tiles_ref.shape[1:3]
    devices = rows_ref.shape[0]
    per_device = own_rows // tile_len
    spare = acc.shape[0] - tile_len
    acc[...] = jnp.zeros_like(acc)
    pick = lax.rem(own_or_other("xl", own) + lax.axis_index("xh"), 2)
    for side, ref in enumerate((tiles_ref, others_ref)):
        core = own_or_other("core", side == 0)
        first = (2 * side + pick) * slots
        count = coords_ref[2, first]
        for t in range(slots):
            cell = coords_ref[0, first + t]
            net = jnp.where(t < count, coords_ref[1, first + t] * tile_len, spare)
            net = pl.multiple_of(net, tile_len)
            row = pl.multiple_of(lax.rem(cell, per_device) * tile_len, tile_len)
            source = core * (devices // 2) + lax.div(cell, per_device)
            cells = rows_ref[source, pl.ds(row, tile_len), :]
            acc[pl.ds(net, tile_len), :] += mxu(ref[pick, t].T, cells, ((1,), (0,)))


def own_or_other(axis, own):
    index = lax.axis_index(axis)
    return index if own else 1 - index


def send_kernel(own_rows, coords_ref, rows_ref, tiles_ref, others_ref, send_ref, acc):
    add_net_sums(coords_ref, rows_ref, tiles_ref, others_ref, acc, False, own_rows)
    send_ref[...] = acc[: send_ref.shape[0], :].astype(send_ref.dtype)


def keep_kernel(own_rows, coords_ref, rows_ref, tiles_ref, others_ref, keep_ref, weight_ref, acc):
    add_net_sums(coords_ref, rows_ref, tiles_ref, others_ref, acc, True, own_rows)
    keep_ref[...] = acc[: keep_ref.shape[0], :]
    depth, few, _ = weight_ref.shape
    weight = rows_ref[0, own_rows:, :].astype(jnp.float32)
    for i in range(1, rows_ref.shape[0]):
        weight = weight + rows_ref[i, own_rows:, :].astype(jnp.float32)
    for z in range(depth):
        weight_ref[z] = weight[z * few : (z + 1) * few].astype(weight_ref.dtype)


def pack_kernel(keep_ref, came_ref, weight_ref, out_ref):
    depth = out_ref.shape[0]
    rows = keep_ref.shape[0] // depth
    for z in range(depth):
        span = slice(z * rows, (z + 1) * rows)
        summed = keep_ref[span, :] + came_ref[span, :].astype(jnp.float32)
        out_ref[z, :rows, :] = summed.astype(out_ref.dtype)
        out_ref[z, rows:, :] = weight_ref[z]


def cell_kernel(
    coords_ref, mine_ref, other_ref, tiles_ref, others_ref, out_hbm, nets, acc, out_ref, sems
):
    depth, lines, _ = mine_ref.shape
    slots, tile_len = tiles_ref.shape[1:3]
    block_nets = nets.shape[0] // 2
    rows = block_nets // depth
    for side, ref in enumerate((mine_ref, other_ref)):
        first = own_or_other("xl", side == 0) * block_nets
        for z in range(depth):
            start = pl.multiple_of(first + z * rows, rows)
            nets[pl.ds(start, rows), :] = ref[z, :rows, :]
    devices = out_ref.shape[0]
    count = devices // 2
    spare = acc.shape[0] - 1
    per_device = spare // count
    few = lines - rows
    for z in range(depth):
        summed = mine_ref[z, rows:, :].astype(jnp.float32)
        summed = (summed + other_ref[z, rows:, :].astype(jnp.float32)).astype(out_ref.dtype)
        line = per_device * tile_len + z * few
        for i in range(devices):
            out_ref[i, line : line + few, :] = summed
    copies = []
    for side, ref in enumerate((tiles_ref, others_ref)):
        core = own_or_other("core", side == 0)
        acc[...] = jnp.zeros_like(acc)
        for pair in range(2):
            high = own_or_other("xh", pair == 0)
            first = (2 * side + pair) * slots
            live = coords_ref[2, first]
            for t in range(slots):
                cell = jnp.where(t < live, coords_ref[0, first + t], spare)
                net = high * block_nets + coords_ref[1, first + t] * tile_len
                net = pl.multiple_of(net, tile_len)
                acc[cell] += mxu(ref[pair, t], nets[pl.ds(net, tile_len), :], ((1,), (0,)))
        for i in range(count):
            at = side * count + i
            for j in range(per_device):
                span = slice(j * tile_len, (j + 1) * tile_len)
                out_ref[at, span, :] = acc[i * per_device + j].astype(out_ref.dtype)
            copies.append(
                pltpu.make_async_copy(out_ref.at[at], out_hbm.at[core * count + i], sems.at[at])
            )
            copies[-1].start()
    for copy in copies:
        copy.wait()


def tail_kernel(terms_ref, root_ref, cells_ref, weight_ref):
    devices, lines, part = terms_ref.shape
    rows, features = cells_ref.shape
    parts = features // part
    count, share = devices // parts, (lines - rows) // parts
    for q in range(parts):
        span = slice(q * part, (q + 1) * part)
        total = terms_ref[q * count, :rows, :].astype(jnp.float32)
        for i in range(1, count):
            total = total + terms_ref[q * count + i, :rows, :].astype(jnp.float32)
        cells_ref[:, span] = (total / root_ref[...]).astype(cells_ref.dtype)
        for i in range(devices):
            first = rows + q * share
            weight_ref[i * share : (i + 1) * share, span] = terms_ref[i, first : first + share, :]


def swap(x, axis):
    return lax.ppermute(x, axis, SWAP)


def exchange(x, axes):
    return lax.all_to_all(x, axes, 0, 0)


def tie(*values):
    return lax.optimization_barrier(values)


def shards(
    grad_out,
    saved_agg,
    theta,
    tile_values,
    tile_coords,
    block_tile_count,
    cell_degree,
    net_pin_count,
):
    own_rows, features = grad_out.shape
    block_cells = cell_degree.shape[0]
    block_nets = net_pin_count.shape[0]
    slots, tile_len = tile_values.shape[2], tile_values.shape[3]
    parts = 4
    part = features // parts
    depth = lax.axis_size("z")
    devices = lax.axis_size(PLANE)
    share_rows = block_nets // depth
    weight_lines = features // devices * parts
    few = weight_lines // depth
    lines = own_rows + weight_lines
    shape = jax.ShapeDtypeStruct
    narrow, wide = jnp.bfloat16, jnp.float32
    net_position = lax.axis_index(NETS)
    low, high = lax.axis_index("xl"), lax.axis_index("xh")

    tiles = tile_values[0]
    tiles = jnp.concatenate([tiles, swap(tiles, "xh")])
    sent = kernel_call(
        head_kernel,
        "head",
        shape((devices, lines, part), narrow),
        [
            pltpu.VMEM((own_rows, features), narrow),
            pltpu.VMEM((features, features), narrow),
            pltpu.VMEM((own_rows, features), narrow),
            pltpu.VMEM((1, block_cells), jnp.int32),
            pltpu.VMEM((parts, own_rows, part), narrow),
            pltpu.VMEM((devices, weight_lines, part), narrow),
            pltpu.SemaphoreType.DMA((4,)),
            pltpu.SemaphoreType.DMA((2, devices)),
        ],
        4 * own_rows * features * features,
        4 << 20,
        [HBM, HBM, HBM, HBM],
        out_specs=HBM,
        vmem=60,
    )(grad_out, theta, saved_agg, cell_degree.reshape(1, block_cells))
    tile_coords, block_tile_count, sent = tie(tile_coords, block_tile_count, sent)
    gathered = exchange(sent, PLANE)

    own = jnp.concatenate(
        [tile_coords[0, 0].T, jnp.broadcast_to(block_tile_count, (1, slots))]
    )
    across = lax.ppermute(own, ("core", "xh"), [(i, 3 - i) for i in range(4)])
    coords = jnp.concatenate([own, swap(own, "xh"), swap(own, "core"), across], axis=1)
    others = swap(tiles, "core")
    own_degree = lax.dynamic_slice_in_dim(cell_degree, net_position * own_rows, own_rows)
    own_root = jnp.sqrt(own_degree.astype(wide))[:, None]
    gathered, tiles, others, coords, own_root = tie(gathered, tiles, others, coords, own_root)

    def net_sums(body, name, outs):
        return kernel_call(
            functools.partial(body, own_rows),
            name,
            outs,
            [pltpu.VMEM((block_nets + tile_len, part), wide)],
            4 * slots * tile_len * tile_len * part,
            3 << 20,
            [SMEM, VMEM, VMEM, VMEM],
        )(coords, gathered, tiles, others)

    sent = net_sums(send_kernel, "sent_sums", shape((block_nets, part), narrow))
    came = swap(sent, "xl")
    keep, weight = net_sums(
        keep_kernel,
        "kept_sums",
        (shape((block_nets, part), wide), shape((depth, few, part), narrow)),
    )
    came, keep = tie(came, keep)
    terms = kernel_call(
        pack_kernel,
        "pack",
        shape((depth, share_rows + few, part), narrow),
        [],
        0,
        1 << 20,
        [VMEM, VMEM, VMEM],
    )(keep, came, weight)
    net_pin_count, terms = tie(net_pin_count, terms)
    summed = exchange(terms, "z")
    pins = jnp.where(low == high, net_pin_count, swap(net_pin_count, "xh"))
    pins = pins.astype(wide).reshape(depth, share_rows)
    pins = lax.dynamic_index_in_dim(pins, lax.axis_index("z"), 0, False)[:, None]
    divisor = jnp.concatenate([pins, jnp.ones((few, 1), wide)], axis=0)
    summed, divisor = tie(summed, divisor)
    summed = jnp.sum(summed.astype(wide), axis=0)
    share = (summed / divisor).astype(narrow)
    mine = exchange(jnp.broadcast_to(share[None], terms.shape), "z")
    other = swap(mine, "xl")
    cell_terms = kernel_call(
        cell_kernel,
        "cell_terms",
        shape((devices, lines, part), narrow),
        [
            pltpu.VMEM((2 * block_nets, part), narrow),
            pltpu.VMEM((block_cells // tile_len + 1, tile_len, part), wide),
            pltpu.VMEM((devices, lines, part), narrow),
            pltpu.SemaphoreType.DMA((devices,)),
        ],
        8 * slots * tile_len * tile_len * part,
        4 << 20,
        [SMEM, VMEM, VMEM, VMEM, VMEM],
        out_specs=HBM,
        vmem=40,
    )(coords, mine, other, tiles, others)
    return kernel_call(
        tail_kernel,
        "tail",
        (shape(grad_out.shape, narrow), shape((features, features), narrow)),
        [],
        0,
        4 << 20,
        [VMEM, VMEM],
    )(exchange(cell_terms, PLANE), own_root)


def solution(mesh):
    cells, nets = mesh.devices.shape
    fine = Mesh(mesh.devices.reshape(cells // 4, 2, 2, 2, nets // 2), CELLS + NETS)
    every = CELLS + NETS
    in_specs = (
        P(every, None),
        P(every, None),
        P(),
        P(CELLS, NETS, None, None, None),
        P(CELLS, NETS, None, None),
        P(CELLS, NETS),
        P(CELLS),
        P(NETS),
    )
    out_specs = (P(every, None), P())
    return jax.shard_map(shards, mesh=fine, in_specs=in_specs, out_specs=out_specs, check_vma=False)
```

```python
import functools

import jax
import jax.numpy as jnp
from jax import lax
from jax.experimental import pallas as pl
from jax.experimental.pallas import tpu as pltpu
from jax.sharding import Mesh
from jax.sharding import PartitionSpec as P

SWAP = ((0, 1), (1, 0))
CELLS = ("z", "xl", "core")
NETS = ("xh", "y")
PLANE = ("core",) + NETS
SMEM = pl.BlockSpec(memory_space=pltpu.SMEM)
VMEM = pl.BlockSpec(memory_space=pltpu.VMEM)
HBM = pl.BlockSpec(memory_space=pltpu.HBM)


def kernel_call(body, name, outs, scratch, flops, nbytes, ins, **grid):
    return pl.pallas_call(
        body,
        out_shape=outs,
        in_specs=ins,
        scratch_shapes=scratch,
        compiler_params=pltpu.CompilerParams(vmem_limit_bytes=grid.pop("vmem", 40) << 20),
        cost_estimate=pl.CostEstimate(flops=flops, bytes_accessed=nbytes, transcendentals=0),
        name=name,
        **({"out_specs": jax.tree.map(lambda _: VMEM, outs)} | grid),
    )


def mxu(a, b, dims):
    return lax.dot_general(a, b, (dims, ((), ())), preferred_element_type=jnp.float32)


def head_kernel(
    grad_hbm,
    theta_hbm,
    saved_hbm,
    degree_hbm,
    out_hbm,
    grad_ref,
    theta_ref,
    saved_ref,
    degree_ref,
    scaled_ref,
    weight_ref,
    in_sems,
    out_sems,
):
    rows, features = grad_ref.shape
    parts, _, part = scaled_ref.shape
    devices, weight_lines, _ = weight_ref.shape
    count, share = devices // parts, weight_lines // parts
    loads = [
        pltpu.make_async_copy(source, target, in_sems.at[i])
        for i, (source, target) in enumerate(
            (
                (degree_hbm, degree_ref),
                (grad_hbm, grad_ref),
                (theta_hbm, theta_ref),
                (saved_hbm, saved_ref),
            )
        )
    ]
    for load in loads:
        load.start()
    loads[0].wait()
    position = lax.axis_index("xh") * lax.axis_size("y") + lax.axis_index("y")
    start = pl.multiple_of(position * rows, rows)
    degree = degree_ref[:, pl.ds(start, rows)].astype(jnp.float32)
    down = lax.broadcasted_iota(jnp.int32, (rows, rows), 0)
    across = lax.broadcasted_iota(jnp.int32, (rows, rows), 1)
    column = jnp.sum(jnp.where(down == across, degree, 0.0), axis=1, keepdims=True)
    root = jnp.sqrt(column)
    loads[1].wait()
    loads[2].wait()
    stores = []

    def store(source, i, first, size, kind):
        stores.append(
            pltpu.make_async_copy(
                source, out_hbm.at[i, pl.ds(first, size), :], out_sems.at[kind, i]
            )
        )
        stores[-1].start()

    scaled = (mxu(grad_ref[...], theta_ref[...], ((1,), (1,))) / root).astype(scaled_ref.dtype)
    for q in range(parts):
        scaled_ref[q] = scaled[:, q * part : (q + 1) * part]
        for i in range(count):
            store(scaled_ref.at[q], q * count + i, 0, rows, 0)
    loads[3].wait()
    terms = mxu(saved_ref[...], grad_ref[...], ((0,), (0,))).astype(weight_ref.dtype)
    for i in range(devices):
        for q in range(parts):
            weight_ref[i, q * share : (q + 1) * share, :] = terms[
                i * share : (i + 1) * share, q * part : (q + 1) * part
            ]
        store(weight_ref.at[i], i, rows, weight_lines, 1)
    for copy in stores:
        copy.wait()


def own_or_other(axis, own):
    index = lax.axis_index(axis)
    return index if own else 1 - index


def add_net_sums(coords_ref, rows_ref, tiles_ref, others_ref, acc, own, own_rows):
    slots, tile_len = tiles_ref.shape[1:3]
    devices = rows_ref.shape[0]
    per_device = own_rows // tile_len
    spare = acc.shape[0] - tile_len
    acc[...] = jnp.zeros_like(acc)
    pick = lax.rem(own_or_other("xl", own) + lax.axis_index("xh"), 2)
    for side, ref in enumerate((tiles_ref, others_ref)):
        core = own_or_other("core", side == 0)
        first = (2 * side + pick) * slots
        count = coords_ref[2, first]
        for t in range(slots):
            cell = coords_ref[0, first + t]
            net = jnp.where(t < count, coords_ref[1, first + t] * tile_len, spare)
            net = pl.multiple_of(net, tile_len)
            row = pl.multiple_of(lax.rem(cell, per_device) * tile_len, tile_len)
            source = core * (devices // 2) + lax.div(cell, per_device)
            cells = rows_ref[source, pl.ds(row, tile_len), :]
            acc[pl.ds(net, tile_len), :] += mxu(ref[pick, t].T, cells, ((1,), (0,)))


def own_or_other(axis, own):
    index = lax.axis_index(axis)
    return index if own else 1 - index


def send_kernel(own_rows, coords_ref, rows_ref, tiles_ref, others_ref, send_ref, acc):
    add_net_sums(coords_ref, rows_ref, tiles_ref, others_ref, acc, False, own_rows)
    send_ref[...] = acc[: send_ref.shape[0], :].astype(send_ref.dtype)


def keep_kernel(own_rows, coords_ref, rows_ref, tiles_ref, others_ref, keep_ref, weight_ref, acc):
    add_net_sums(coords_ref, rows_ref, tiles_ref, others_ref, acc, True, own_rows)
    keep_ref[...] = acc[: keep_ref.shape[0], :]
    depth, few, _ = weight_ref.shape
    weight = rows_ref[0, own_rows:, :].astype(jnp.float32)
    for i in range(1, rows_ref.shape[0]):
        weight = weight + rows_ref[i, own_rows:, :].astype(jnp.float32)
    for z in range(depth):
        weight_ref[z] = weight[z * few : (z + 1) * few].astype(weight_ref.dtype)


def pack_kernel(keep_ref, came_ref, weight_ref, out_ref):
    depth = out_ref.shape[0]
    rows = keep_ref.shape[0] // depth
    for z in range(depth):
        span = slice(z * rows, (z + 1) * rows)
        summed = keep_ref[span, :] + came_ref[span, :].astype(jnp.float32)
        out_ref[z, :rows, :] = summed.astype(out_ref.dtype)
        out_ref[z, rows:, :] = weight_ref[z]


def cell_kernel(
    coords_ref, mine_ref, other_ref, tiles_ref, others_ref, out_hbm, nets, acc, out_ref, sems
):
    depth, lines, _ = mine_ref.shape
    slots, tile_len = tiles_ref.shape[1:3]
    block_nets = nets.shape[0] // 2
    rows = block_nets // depth
    for side, ref in enumerate((mine_ref, other_ref)):
        first = own_or_other("xl", side == 0) * block_nets
        for z in range(depth):
            start = pl.multiple_of(first + z * rows, rows)
            nets[pl.ds(start, rows), :] = ref[z, :rows, :]
    devices = out_ref.shape[0]
    count = devices // 2
    spare = acc.shape[0] - 1
    per_device = spare // count
    few = lines - rows
    for z in range(depth):
        summed = mine_ref[z, rows:, :].astype(jnp.float32)
        summed = (summed + other_ref[z, rows:, :].astype(jnp.float32)).astype(out_ref.dtype)
        line = per_device * tile_len + z * few
        for i in range(devices):
            out_ref[i, line : line + few, :] = summed
    copies = []
    for side, ref in enumerate((tiles_ref, others_ref)):
        core = own_or_other("core", side == 0)
        acc[...] = jnp.zeros_like(acc)
        for pair in range(2):
            high = own_or_other("xh", pair == 0)
            first = (2 * side + pair) * slots
            live = coords_ref[2, first]
            for t in range(slots):
                cell = jnp.where(t < live, coords_ref[0, first + t], spare)
                net = high * block_nets + coords_ref[1, first + t] * tile_len
                net = pl.multiple_of(net, tile_len)
                acc[cell] += mxu(ref[pair, t], nets[pl.ds(net, tile_len), :], ((1,), (0,)))
        for i in range(count):
            at = side * count + i
            for j in range(per_device):
                span = slice(j * tile_len, (j + 1) * tile_len)
                out_ref[at, span, :] = acc[i * per_device + j].astype(out_ref.dtype)
            copies.append(
                pltpu.make_async_copy(out_ref.at[at], out_hbm.at[core * count + i], sems.at[at])
            )
            copies[-1].start()
    for copy in copies:
        copy.wait()


def tail_kernel(terms_ref, root_ref, cells_ref, weight_ref):
    devices, lines, part = terms_ref.shape
    rows, features = cells_ref.shape
    parts = features // part
    count, share = devices // parts, (lines - rows) // parts
    for q in range(parts):
        span = slice(q * part, (q + 1) * part)
        total = terms_ref[q * count, :rows, :].astype(jnp.float32)
        for i in range(1, count):
            total = total + terms_ref[q * count + i, :rows, :].astype(jnp.float32)
        cells_ref[:, span] = (total / root_ref[...]).astype(cells_ref.dtype)
        for i in range(devices):
            first = rows + q * share
            weight_ref[i * share : (i + 1) * share, span] = terms_ref[i, first : first + share, :]


def swap(x, axis):
    return lax.ppermute(x, axis, SWAP)


def exchange(x, axes):
    return lax.all_to_all(x, axes, 0, 0)


def tie(*values):
    return lax.optimization_barrier(values)


def shards(
    grad_out,
    saved_agg,
    theta,
    tile_values,
    tile_coords,
    block_tile_count,
    cell_degree,
    net_pin_count,
):
    own_rows, features = grad_out.shape
    block_cells = cell_degree.shape[0]
    block_nets = net_pin_count.shape[0]
    slots, tile_len = tile_values.shape[2], tile_values.shape[3]
    parts = 4
    part = features // parts
    depth = lax.axis_size("z")
    devices = lax.axis_size(PLANE)
    share_rows = block_nets // depth
    weight_lines = features // devices * parts
    few = weight_lines // depth
    lines = own_rows + weight_lines
    shape = jax.ShapeDtypeStruct
    narrow, wide = jnp.bfloat16, jnp.float32
    net_position = lax.axis_index(NETS)
    low, high = lax.axis_index("xl"), lax.axis_index("xh")

    tiles = tile_values[0]
    tiles = jnp.concatenate([tiles, swap(tiles, "xh")])
    sent = kernel_call(
        head_kernel,
        "head",
        shape((devices, lines, part), narrow),
        [
            pltpu.VMEM((own_rows, features), narrow),
            pltpu.VMEM((features, features), narrow),
            pltpu.VMEM((own_rows, features), narrow),
            pltpu.VMEM((1, block_cells), jnp.int32),
            pltpu.VMEM((parts, own_rows, part), narrow),
            pltpu.VMEM((devices, weight_lines, part), narrow),
            pltpu.SemaphoreType.DMA((4,)),
            pltpu.SemaphoreType.DMA((2, devices)),
        ],
        4 * own_rows * features * features,
        4 << 20,
        [HBM, HBM, HBM, HBM],
        out_specs=HBM,
        vmem=60,
    )(grad_out, theta, saved_agg, cell_degree.reshape(1, block_cells))
    tile_coords, block_tile_count, net_pin_count, sent = tie(
        tile_coords, block_tile_count, net_pin_count, sent
    )
    gathered = exchange(sent, PLANE)

    own = jnp.concatenate(
        [tile_coords[0, 0].T, jnp.broadcast_to(block_tile_count, (1, slots))]
    )
    across = lax.ppermute(own, ("core", "xh"), [(i, 3 - i) for i in range(4)])
    coords = jnp.concatenate([own, swap(own, "xh"), swap(own, "core"), across], axis=1)
    others = swap(tiles, "core")
    pins = jnp.where(low == high, net_pin_count, swap(net_pin_count, "xh"))
    pins = pins.astype(wide).reshape(depth, share_rows)
    pins = lax.dynamic_index_in_dim(pins, lax.axis_index("z"), 0, False)[:, None]
    divisor = jnp.concatenate([pins, jnp.ones((few, 1), wide)], axis=0)
    own_degree = lax.dynamic_slice_in_dim(cell_degree, net_position * own_rows, own_rows)
    own_root = jnp.sqrt(own_degree.astype(wide))[:, None]
    gathered, tiles, others, coords, own_root = tie(gathered, tiles, others, coords, own_root)

    def net_sums(body, name, outs):
        return kernel_call(
            functools.partial(body, own_rows),
            name,
            outs,
            [pltpu.VMEM((block_nets + tile_len, part), wide)],
            4 * slots * tile_len * tile_len * part,
            3 << 20,
            [SMEM, VMEM, VMEM, VMEM],
        )(coords, gathered, tiles, others)

    sent = net_sums(send_kernel, "sent_sums", shape((block_nets, part), narrow))
    came = swap(sent, "xl")
    keep, weight = net_sums(
        keep_kernel,
        "kept_sums",
        (shape((block_nets, part), wide), shape((depth, few, part), narrow)),
    )
    came, keep, divisor = tie(came, keep, divisor)
    terms = kernel_call(
        pack_kernel,
        "pack",
        shape((depth, share_rows + few, part), narrow),
        [],
        0,
        1 << 20,
        [VMEM, VMEM, VMEM],
    )(keep, came, weight)
    summed = exchange(terms, "z")
    summed = jnp.sum(summed.astype(wide), axis=0)
    share = (summed / divisor).astype(narrow)
    mine = exchange(jnp.broadcast_to(share[None], terms.shape), "z")
    other = swap(mine, "xl")
    cell_terms = kernel_call(
        cell_kernel,
        "cell_terms",
        shape((devices, lines, part), narrow),
        [
            pltpu.VMEM((2 * block_nets, part), narrow),
            pltpu.VMEM((block_cells // tile_len + 1, tile_len, part), wide),
            pltpu.VMEM((devices, lines, part), narrow),
            pltpu.SemaphoreType.DMA((devices,)),
        ],
        8 * slots * tile_len * tile_len * part,
        4 << 20,
        [SMEM, VMEM, VMEM, VMEM, VMEM],
        out_specs=HBM,
        vmem=40,
    )(coords, mine, other, tiles, others)
    return kernel_call(
        tail_kernel,
        "tail",
        (shape(grad_out.shape, narrow), shape((features, features), narrow)),
        [],
        0,
        4 << 20,
        [VMEM, VMEM],
    )(exchange(cell_terms, PLANE), own_root)


def solution(mesh):
    cells, nets = mesh.devices.shape
    fine = Mesh(mesh.devices.reshape(cells // 4, 2, 2, 2, nets // 2), CELLS + NETS)
    every = CELLS + NETS
    in_specs = (
        P(every, None),
        P(every, None),
        P(),
        P(CELLS, NETS, None, None, None),
        P(CELLS, NETS, None, None),
        P(CELLS, NETS),
        P(CELLS),
        P(NETS),
    )
    out_specs = (P(every, None), P())
    return jax.shard_map(shards, mesh=fine, in_specs=in_specs, out_specs=out_specs, check_vma=False)
```
